32 devices in a mesh: dp: 16 (over z, y, x), tensor: 2 (over core).
Axes of the slice: x: 2, y: 2, z: 4, core: 2. Of those that a mesh axis runs over, the one named last changes fastest.
Arguments:
- block_input: bfloat16 [8192, 768], P('dp'), may hold values from -6 to 6
- sequence_ids: int32 [8192], P('dp'), may hold values from 0 to 1, as said below
- attention_gain: float32 [768], replicated, may hold values from 0.25 to 1.75
- attention_shift: float32 [768], replicated, may hold values from -2 to 2
- packed_weight: bfloat16 [768, 3, 768], P(None, None, 'tensor'), may hold values from -0.21875 to 0.21875
- packed_bias: float32 [3, 768], P(None, 'tensor'), may hold values from -3 to 3
- output_weight: bfloat16 [768, 768], P('tensor'), may hold values from -1.75 to 1.75
- output_bias: float32 [768], replicated, may hold values from -3 to 3
- feedforward_gain: float32 [768], replicated, may hold values from 0.25 to 1.75
- feedforward_shift: float32 [768], replicated, may hold values from -2 to 2
- expand_weight: bfloat16 [768, 3072], P(None, 'tensor'), may hold values from -0.21875 to 0.21875
- expand_bias: float32 [3072], P('tensor'), may hold values from -3 to 3
- shrink_weight: bfloat16 [3072, 768], P('tensor'), may hold values from -0.109375 to 0.109375
- shrink_bias: float32 [768], replicated, may hold values from -3 to 3
- grad_output: bfloat16 [8192, 768], P('dp'), may hold values from -6 to 6
Outputs:
- block_output: bfloat16 [8192, 768], P('dp')
- grad_input: bfloat16 [8192, 768], P('dp')
- grad_attention_gain: float32 [768], replicated
- grad_attention_shift: float32 [768], replicated
- grad_packed_weight: float32 [768, 3, 768], P(None, None, 'tensor')
- grad_packed_bias: float32 [3, 768], P(None, 'tensor')
- grad_output_weight: float32 [768, 768], P('tensor')
- grad_output_bias: float32 [768], replicated
- grad_feedforward_gain: float32 [768], replicated
- grad_feedforward_shift: float32 [768], replicated
- grad_expand_weight: float32 [768, 3072], P(None, 'tensor')
- grad_expand_bias: float32 [3072], P('tensor')
- grad_shrink_weight: float32 [3072, 768], P('tensor')
- grad_shrink_bias: float32 [768], replicated
The draws below stay inside these ranges and needn't reach their ends.
Inputs may be any that keep to these rules, and one draw needn't show every extreme that they name: `sequence_ids`: in each block of 512 rows along the tokens (the rows of one index of dp), tokens with equal values form one sequence in order: the value is 0 on the first 256 rows, and on the other 256 rows either 0 throughout (one sequence of 512) or 1 throughout (two sequences of 256); the first block is always of the second kind.
All inputs are finite; a program needn't handle non-finite values.
Results may differ from the reference program's by a relative error of at most 0.013.
The reference program's roundings to bfloat16 on the way count: a program that leaves them out, or rounds other values in their place, can miss the bound.
Values sent between devices are 32-bit elements; how exact they have to be, the bound alone decides.
A program may use at most 128 MiB of HBM per device.

```python
import math
import jax
import jax.numpy as jnp
from jax import lax

D = 768
HEADS = 12
HEAD = 64
FF = 3072
SHORT = 256
TOK_DEV = 512
TOKENS = 8192


def draw_sequence_ids(key, part):
    blocks = TOKENS // TOK_DEV
    split_flags = jax.random.randint(key, (blocks,), 0, 2).astype(jnp.int32)
    split_flags = split_flags.at[0].set(1)
    second_half = (jnp.arange(TOK_DEV, dtype=jnp.int32) >= SHORT).astype(jnp.int32)
    return (split_flags[:, None] * second_half[None, :]).reshape(TOKENS).astype(jnp.int32)


def block_scale(rng, dims, cuts, smallest, top_value):
    loudness, own = 1.0, jax.random.fold_in(rng, 6)
    for position, parts in cuts:
        steps = jnp.exp(jax.random.uniform(jax.random.fold_in(own, position), (parts,), jnp.float32, smallest / len(cuts), top_value / len(cuts)))
        loudness = loudness * jnp.repeat(steps, dims[position] // parts).reshape([-1 if axis == position else 1 for axis in range(len(dims))])
    return loudness


def scatter_about(stream_key, dims, width, most, cuts=(), kind=jnp.bfloat16):
    drawn = width * jax.random.normal(stream_key, dims, jnp.float32)
    if cuts:
        drawn = drawn * block_scale(stream_key, dims, cuts, -0.22, 0.18)
    return jnp.clip(drawn, -most, most).astype(kind)


def setup_inputs(seed: int = 0) -> dict:
    streams_of = jax.random.split(jax.random.key(seed), 16)
    return {
        "block_input": scatter_about(streams_of[0], (TOKENS, D), 1.0, 6.0, ((0, 16),)),
        "sequence_ids": draw_sequence_ids(jax.random.fold_in(streams_of[15], 71), 0),
        "attention_gain": jnp.clip(1.0 + 0.15 * jax.random.normal(streams_of[2], (D,), jnp.float32), 0.25, 1.75),
        "attention_shift": scatter_about(streams_of[3], (D,), 0.3, 2.0, (), jnp.float32),
        "packed_weight": scatter_about(streams_of[4], (D, 3, D), D ** -0.5, 0.21875, ((2, 2),)),
        "packed_bias": scatter_about(streams_of[5], (3, D), 0.5, 3.0, ((1, 2),), jnp.float32),
        "output_weight": scatter_about(streams_of[6], (D, D), (max(D // 64, 8)) ** -0.5, 1.75, ((0, 2),)),
        "output_bias": scatter_about(streams_of[7], (D,), 0.5, 3.0, (), jnp.float32),
        "feedforward_gain": jnp.clip(1.0 + 0.15 * jax.random.normal(streams_of[8], (D,), jnp.float32), 0.25, 1.75),
        "feedforward_shift": scatter_about(streams_of[9], (D,), 0.3, 2.0, (), jnp.float32),
        "expand_weight": scatter_about(streams_of[10], (D, FF), D ** -0.5, 0.21875, ((1, 2),)),
        "expand_bias": scatter_about(streams_of[11], (FF,), 0.5, 3.0, ((0, 2),), jnp.float32),
        "shrink_weight": scatter_about(streams_of[12], (FF, D), FF ** -0.5, 0.109375, ((0, 2),)),
        "shrink_bias": scatter_about(streams_of[13], (D,), 0.5, 3.0, (), jnp.float32),
        "grad_output": scatter_about(streams_of[14], (TOKENS, D), 1.0, 6.0, ((0, 16),)),
    }


PRECISE = lax.Precision.HIGHEST
EPSILON = 1e-05
MASKED = -1000000000.0

@jax.custom_vjp
def low(v):
    return lax.optimization_barrier(v.astype(jnp.bfloat16)).astype(jnp.float32)

@jax.custom_vjp
def low_back(v):
    return v

def low_keep(v):
    return (low(v), None)

def low_pass(kept, grad):
    return (grad,)

def back_keep(v):
    return (v, None)

def back_low(kept, grad):
    return (low(grad),)
low.defvjp(low_keep, low_pass)
low_back.defvjp(back_keep, back_low)

def norm_rows(values_in):
    row_mean = lax.optimization_barrier(jnp.mean(values_in, axis=-1, keepdims=True))
    centred = values_in - row_mean
    inv_std = lax.rsqrt(lax.optimization_barrier(jnp.mean(centred * centred, axis=-1, keepdims=True)) + EPSILON)
    return centred * inv_std

def rotary_tables(block_ids, head_size):
    earlier = (block_ids[None, :] < block_ids[:, None]).astype(jnp.int32)
    places = jnp.arange(block_ids.shape[0], dtype=jnp.int32) - lax.optimization_barrier(jnp.sum(earlier, axis=1)).astype(jnp.int32)
    half_size = head_size // 2
    frequency = jnp.exp(jnp.arange(half_size, dtype=jnp.float32) * (-2.0 * math.log(10000.0) / head_size))
    angles = places.astype(jnp.float32)[:, None] * frequency[None, :]
    return (jnp.cos(angles), jnp.sin(angles))

def rotate(heads_in, cosine, sine_part):
    half_size = heads_in.shape[-1] // 2
    front_half = heads_in[..., :half_size]
    back_half = heads_in[..., half_size:]
    cos_rows = cosine[:, None, :]
    sin_rows = sine_part[:, None, :]
    return jnp.concatenate([front_half * cos_rows - back_half * sin_rows, back_half * cos_rows + front_half * sin_rows], axis=-1)

def attend_block(pieces):
    split_heads, block_ids = pieces
    cosine, sine_part = rotary_tables(block_ids, HEAD)
    queries = low(rotate(split_heads[:, 0], cosine, sine_part))
    keys_rot = low(rotate(split_heads[:, 1], cosine, sine_part))
    values_low = low(split_heads[:, 2])
    scores = low_back(jnp.einsum('qhd,khd->hqk', queries, keys_rot, precision=PRECISE) * HEAD ** (-0.5))
    same_sequence = (block_ids[:, None] == block_ids[None, :])[None]
    scores = jnp.where(same_sequence, scores, MASKED)
    row_max = lax.optimization_barrier(jnp.max(scores, axis=-1, keepdims=True))
    log_total = row_max + jnp.log(lax.optimization_barrier(jnp.sum(jnp.exp(scores - row_max), axis=-1, keepdims=True)))
    prob_full = jnp.exp(scores - log_total)
    return low_back(jnp.einsum('hqk,khd->qhd', low(prob_full), values_low, precision=PRECISE))

def layer_group(params, group_input, group_ids):
    attention_gain, attention_shift, packed_weight, packed_bias, output_weight, output_bias, feedforward_gain, feedforward_shift, expand_weight, expand_bias, shrink_weight, shrink_bias = params
    token_count = group_input.shape[0]
    block_count = token_count // TOK_DEV
    attend_in = low(norm_rows(group_input) * attention_gain + attention_shift)
    packed = low_back(jnp.einsum('td,dcw->tcw', attend_in, packed_weight, precision=PRECISE) + packed_bias)
    split_heads = packed.reshape(block_count, TOK_DEV, 3, HEADS, HEAD)
    block_ids = group_ids.reshape(block_count, TOK_DEV)
    attended = lax.map(jax.checkpoint(attend_block), (split_heads, block_ids))
    attended = low(attended.reshape(token_count, D))
    mixed = low_back(jnp.dot(attended, output_weight, precision=PRECISE))
    middle = group_input + mixed + output_bias
    expand_in = low(norm_rows(middle) * feedforward_gain + feedforward_shift)
    pre_act = low_back(jnp.dot(expand_in, expand_weight, precision=PRECISE) + expand_bias)
    act_low = low(jax.nn.gelu(pre_act, approximate=False))
    shrunk = low_back(jnp.dot(act_low, shrink_weight, precision=PRECISE))
    return middle + shrunk + shrink_bias

def reference(block_input, sequence_ids, attention_gain, attention_shift, packed_weight, packed_bias, output_weight, output_bias, feedforward_gain, feedforward_shift, expand_weight, expand_bias, shrink_weight, shrink_bias, grad_output):
    params = (attention_gain.astype(jnp.float32), attention_shift.astype(jnp.float32), packed_weight.astype(jnp.float32), packed_bias.astype(jnp.float32), output_weight.astype(jnp.float32), output_bias.astype(jnp.float32), feedforward_gain.astype(jnp.float32), feedforward_shift.astype(jnp.float32), expand_weight.astype(jnp.float32), expand_bias.astype(jnp.float32), shrink_weight.astype(jnp.float32), shrink_bias.astype(jnp.float32))
    block_count = TOKENS // TOK_DEV
    per_group = max(1, min(block_count, 4096 // TOK_DEV))
    while block_count % per_group != 0:
        per_group = per_group - 1
    group_count = block_count // per_group
    group_rows = per_group * TOK_DEV
    inputs_all = block_input.astype(jnp.float32).reshape(group_count, group_rows, D)
    ids_all = sequence_ids.reshape(group_count, group_rows)
    cotangent = grad_output.astype(jnp.float32).reshape(group_count, group_rows, D)

    def one_group(totals, pieces):
        group_input, group_ids, group_grad = pieces

        def forward(param_set, layer_input):
            return layer_group(param_set, layer_input, group_ids)
        output_rows, pull_back = jax.vjp(forward, params, group_input)
        param_grads, input_grads = pull_back(group_grad)
        summed = jax.tree.map(lambda earlier_sum, added: earlier_sum + added, totals, param_grads)
        return (summed, (output_rows, input_grads))
    empty_grads = jax.tree.map(jnp.zeros_like, params)
    totals, (output_rows, input_grads) = lax.scan(one_group, empty_grads, (inputs_all, ids_all, cotangent))
    return (output_rows.reshape(TOKENS, D).astype(jnp.bfloat16), input_grads.reshape(TOKENS, D).astype(jnp.bfloat16), totals[0], totals[1], totals[2], totals[3], totals[4], totals[5], totals[6], totals[7], totals[8], totals[9], totals[10], totals[11])
```

```python
import functools
import math

import jax
import jax.numpy as jnp
from jax import lax
from jax.experimental import pallas as pl
from jax.experimental.pallas import tpu as pltpu
from jax.sharding import PartitionSpec as P

HEAD = 64


MESH = pl.DeviceIdType.MESH
W = 8
R = 64
LF = 2


class Comm:
    def __init__(self, n, counts, G, O, RF, RU, RD, RL, sems):
        self.nz = n // 4
        self.counts = counts
        self.G, self.O, self.RF, self.RU, self.RD, self.RL = G, O, RF, RU, RD, RL
        self.sems = sems
        d = lax.axis_index("dp")
        self.t = lax.axis_index("tensor")
        self.d = d
        self.z = d // 4
        self.y = (d // 2) % 2
        self.x = d % 2
        self.px = d + 1 - 2 * self.x
        self.py = d + 2 - 4 * self.y

    def steps(self):
        return max(self.counts) + LF + 2 * self.nz + 3

    def barrier(self):
        b = pltpu.get_barrier_semaphore()
        for peer in (self.px, self.py):
            pl.semaphore_signal(b, inc=1, device_id=(peer, self.t), device_id_type=MESH)

        @pl.when(self.z > 0)
        def _():
            pl.semaphore_signal(b, inc=1, device_id=(self.d - 4, self.t), device_id_type=MESH)

        @pl.when(self.z < self.nz - 1)
        def _():
            pl.semaphore_signal(b, inc=1, device_id=(self.d + 4, self.t), device_id_type=MESH)

        edge = (self.z > 0).astype(jnp.int32) + (self.z < self.nz - 1).astype(jnp.int32)
        pl.semaphore_wait(b, 2 + edge)

    def rows(self, start, size):
        return self.G.at[pl.ds(pl.multiple_of(start, 8), size), :]

    def done(self, start, size):
        return self.O.at[pl.ds(pl.multiple_of(start, 8), size), :]

    def copy(self, src, dst, kind, idx, dev):
        return pltpu.make_async_remote_copy(
            src_ref=src, dst_ref=dst, send_sem=self.sems[kind + "s"].at[idx], recv_sem=self.sems[kind + "r"].at[idx],
            device_id=(dev, self.t), device_id_type=MESH)

    def add(self, start, size, buf):
        r = self.rows(start, size)
        r[...] = r[...] + buf[...]

    def step(self, i):
        for c in (0, 1):
            self.first(c, i)
        for c in (0, 1):
            self.rest(c, i)

    def base(self, c, k):
        return (2 * k + c) * R

    def f_copy(self, c, k):
        a, dev = (self.x, self.px) if c == 0 else (self.y, self.py)
        q = k % W
        return self.copy(self.rows(self.base(c, k) + (1 - a) * (R // 2), R // 2), self.RF.at[c, q], "F", (c, q), dev)

    def first(self, c, i):
        @pl.when(i < self.counts[c])
        def _():
            self.f_copy(c, i).start()

    def rest(self, c, i):
        nz, z = self.nz, self.z
        a, fdev, b, ldev = (self.x, self.px, self.y, self.py) if c == 0 else (self.y, self.py, self.x, self.px)
        n = self.counts[c]
        H, Q, E = R // 2, R // 4, R // 8

        def ok(k):
            return (k >= 0) & (k < n)

        def half(k):
            return self.base(c, k) + a * H

        def sub(k, s):
            return half(k) + s * Q

        def root(k, s):
            return k % 2 if s == 0 else nz - 1 - k % 2

        k = i - LF

        @pl.when(ok(k))
        def _(k=k):
            cp = self.f_copy(c, k)
            cp.wait_send()
            cp.wait_recv()
            self.add(half(k), H, self.RF.at[c, k % W])

        def up(k, s):
            return self.copy(self.rows(sub(k, s), Q), self.RU.at[c, s, k % W], "U", (c, s, k % W), jnp.minimum(self.d + 4, 4 * nz - 1))

        def dn(k, s):
            return self.copy(self.rows(sub(k, s), Q), self.RD.at[c, s, k % W], "D", (c, s, k % W), jnp.maximum(self.d - 4, 0))

        for s in (0, 1):
            k = i - (LF + z)

            @pl.when(ok(k) & (z <= root(k, s)) & (z > 0))
            def _(k=k, s=s):
                up(k, s).wait_recv()
                self.add(sub(k, s), Q, self.RU.at[c, s, k % W])

            @pl.when(ok(k) & (z < root(k, s)))
            def _(k=k, s=s):
                up(k, s).start()

            k = i - (LF + nz - 1 - z)

            @pl.when(ok(k) & (z >= root(k, s)) & (z < nz - 1))
            def _(k=k, s=s):
                dn(k, s).wait_recv()
                self.add(sub(k, s), Q, self.RD.at[c, s, k % W])

            @pl.when(ok(k) & (z > root(k, s)))
            def _(k=k, s=s):
                dn(k, s).start()

            k = i - (LF + z + 1)

            @pl.when(ok(k) & (z < root(k, s)))
            def _(k=k, s=s):
                up(k, s).wait_send()

            k = i - (LF + nz - 1 - z + 1)

            @pl.when(ok(k) & (z > root(k, s)))
            def _(k=k, s=s):
                dn(k, s).wait_send()

        def last(k, s):
            return self.copy(self.rows(sub(k, s) + (1 - b) * E, E), self.RL.at[c, k % W], "L", (c, k % W), ldev)

        def last_back(k, s):
            at = sub(k, s) + b * E
            return self.copy(self.rows(at, E), self.done(at, E), "M", (c, k % W), ldev)

        for s in (0, 1):
            k = i - (LF + nz - 1)

            @pl.when(ok(k) & (z == root(k, s)))
            def _(k=k, s=s):
                last(k, s).start()

            k = i - (LF + nz)

            @pl.when(ok(k) & (z == root(k, s)))
            def _(k=k, s=s):
                cp = last(k, s)
                cp.wait_send()
                cp.wait_recv()
                self.add(sub(k, s) + b * E, E, self.RL.at[c, k % W])
                last_back(k, s).start()
                self.done(sub(k, s) + b * E, E)[...] = self.rows(sub(k, s) + b * E, E)[...]

        def g_up(k, s):
            r = self.done(sub(k, s), Q)
            return self.copy(r, r, "V", (c, s, k % W), jnp.minimum(self.d + 4, 4 * nz - 1))

        def g_dn(k, s):
            r = self.done(sub(k, s), Q)
            return self.copy(r, r, "E", (c, s, k % W), jnp.maximum(self.d - 4, 0))

        def g_first(k, s):
            r = self.done(sub(k, s), Q)
            return self.copy(r, r, "G", (c, s, k % W), fdev)

        for e in (0, 1):
            for s in (0, 1):
                r = e if s == 0 else nz - 1 - e
                lag = LF + nz + 1 + jnp.abs(z - r)
                k = i - lag
                here = ok(k) & (k % 2 == e)

                @pl.when(here & (z == r))
                def _(k=k, s=s):
                    cp = last_back(k, s)
                    cp.wait_send()
                    cp.wait_recv()

                @pl.when(here & (z < r))
                def _(k=k, s=s):
                    g_dn(k, s).wait_recv()

                @pl.when(here & (z > r))
                def _(k=k, s=s):
                    g_up(k, s).wait_recv()

                @pl.when(here & (z <= r) & (z > 0))
                def _(k=k, s=s):
                    g_dn(k, s).start()

                @pl.when(here & (z >= r) & (z < nz - 1))
                def _(k=k, s=s):
                    g_up(k, s).start()

                @pl.when(here)
                def _(k=k, s=s):
                    g_first(k, s).start()

                k = i - (lag + 1)
                here = ok(k) & (k % 2 == e)

                @pl.when(here)
                def _(k=k, s=s):
                    cp = g_first(k, s)
                    cp.wait_send()
                    cp.wait_recv()

                @pl.when(here & (z <= r) & (z > 0))
                def _(k=k, s=s):
                    g_dn(k, s).wait_send()

                @pl.when(here & (z >= r) & (z < nz - 1))
                def _(k=k, s=s):
                    g_up(k, s).wait_send()


KINDS = {"F": (2, W), "U": (2, 2, W), "D": (2, 2, W), "L": (2, W), "M": (2, W), "V": (2, 2, W), "E": (2, 2, W), "G": (2, 2, W)}
SEMS = [k + e for k in KINDS for e in "sr"]


def comm_scratch(width):
    return [
        pltpu.VMEM((2, W, R // 2, width), jnp.float32),
        pltpu.VMEM((2, 2, W, R // 4, width), jnp.float32),
        pltpu.VMEM((2, 2, W, R // 4, width), jnp.float32),
        pltpu.VMEM((2, W, R // 8, width), jnp.float32),
    ] + [pltpu.SemaphoreType.DMA(KINDS[k[0]]) for k in SEMS]


def pieces_of(width, hidden, heads_width):
    out = []
    row = 0
    out.append((row, 0, 0, 0, hidden, width, 0))
    row += hidden
    for part in range(hidden // width):
        out.append((row, 1, 0, part * width, width, width, 0))
        row += width
    out.append((row, 2, 0, 0, heads_width, width, 0))
    row += heads_width
    for part in range(2):
        out.append((row, 3, 0, part * heads_width, width, heads_width, part * heads_width))
    row += width
    for part in range(2):
        out.append((row, 3, part * heads_width, 2 * heads_width, heads_width, heads_width, part * heads_width))
    row += heads_width
    out.append((row, 4, 0, 0, R, width, 0))
    row += R
    return out, row


def moves(arrays, whole, blocks, local, out):
    made = []
    for j, (row, which, r0, c0, nr, nc, g0) in enumerate(blocks):
        here = whole.at[pl.ds(row, nr), pl.ds(g0, nc)]
        there = arrays[which]
        if len(there.shape) == 3:
            there = there.at[c0 // nc]
            c0 = 0
        there = there.at[pl.ds(r0, nr), pl.ds(c0, nc)]
        pair = (here, there) if out else (there, here)
        made.append(pltpu.make_async_copy(*pair, local.at[j]))
    return made


def sum_kernel(n, blocks, total, *refs):
    ins, O = refs[:5], refs[5]
    G, RF, RU, RD, RL, local = refs[6:12]
    sems = dict(zip(SEMS, refs[12:]))
    full = (total - R) // (2 * R)
    comm = Comm(n, (full + 1, full), G, O, RF, RU, RD, RL, sems)
    loads = moves(ins, G, blocks, local, False)
    for cp in loads:
        cp.start()
    comm.barrier()
    for cp in loads:
        cp.wait()

    def body(i, carry):
        comm.step(i)
        return carry

    lax.fori_loop(0, comm.steps(), body, 0)


def unpack_kernel(blocks, whole, *refs):
    stores = moves(refs[:5], whole, blocks, refs[5], True)
    for cp in stores:
        cp.start()
    for cp in stores:
        cp.wait()


def sum_grads(n, arrays, width, hidden, heads_width):
    blocks, total = pieces_of(width, hidden, heads_width)
    anywhere = pl.BlockSpec(memory_space=pl.ANY)
    scratch = comm_scratch(width)
    local = pltpu.SemaphoreType.DMA((len(blocks),))
    summed = pl.pallas_call(
        functools.partial(sum_kernel, n, blocks, total),
        out_shape=pltpu.VMEM((total, width), jnp.float32),
        in_specs=[anywhere] * 5,
        out_specs=pl.BlockSpec(memory_space=pltpu.VMEM),
        scratch_shapes=[pltpu.VMEM((total, width), jnp.float32)] + scratch[:4] + [local] + scratch[4:],
        compiler_params=pltpu.CompilerParams(
            collective_id=0, has_side_effects=True, vmem_limit_bytes=26 << 20
        ),
    )(*arrays)
    return pl.pallas_call(
        functools.partial(unpack_kernel, blocks),
        out_shape=[pltpu.HBM(a.shape, jnp.float32) for a in arrays],
        in_specs=[anywhere],
        out_specs=[anywhere] * 5,
        scratch_shapes=[local],
        compiler_params=pltpu.CompilerParams(vmem_limit_bytes=1 << 20),
    )(summed)


EPSILON = 1e-05
MASKED = -1000000000.0


def norm_rows(values_in):
    row_mean = jnp.mean(values_in, axis=-1, keepdims=True)
    centred = values_in - row_mean
    inv_std = lax.rsqrt(jnp.mean(centred * centred, axis=-1, keepdims=True) + EPSILON)
    return (centred * inv_std, inv_std)


def norm_back(grad_normed, normed, inv_std, gain_vector):
    scaled = grad_normed * gain_vector
    centred = scaled - jnp.mean(scaled, axis=-1, keepdims=True)
    return (centred - normed * jnp.mean(scaled * normed, axis=-1, keepdims=True)) * inv_std


def rotary_tables(block_ids, head_size):
    earlier = (block_ids[None, :] < block_ids[:, None]).astype(jnp.int32)
    places = jnp.arange(block_ids.shape[0], dtype=jnp.int32) - jnp.sum(earlier, axis=1)
    half_size = head_size // 2
    frequency = jnp.exp(
        jnp.arange(half_size, dtype=jnp.float32) * (-2.0 * math.log(10000.0) / head_size)
    )
    angles = places.astype(jnp.float32)[:, None] * frequency[None, :]
    return (jnp.cos(angles), jnp.sin(angles))


def rotate(heads_in, cosine, sine_part):
    half_size = heads_in.shape[-1] // 2
    front_half = heads_in[..., :half_size]
    back_half = heads_in[..., half_size:]
    cos_rows = cosine[:, None, :]
    sin_rows = sine_part[:, None, :]
    return jnp.concatenate(
        [
            front_half * cos_rows - back_half * sin_rows,
            back_half * cos_rows + front_half * sin_rows,
        ],
        axis=-1,
    )


def rotate_back(grads_in, cosine, sine_part):
    half_size = grads_in.shape[-1] // 2
    front_half = grads_in[..., :half_size]
    back_half = grads_in[..., half_size:]
    cos_rows = cosine[:, None, :]
    sin_rows = sine_part[:, None, :]
    return jnp.concatenate(
        [
            front_half * cos_rows + back_half * sin_rows,
            back_half * cos_rows - front_half * sin_rows,
        ],
        axis=-1,
    )


def body(
    n_dp,
    block_input,
    sequence_ids,
    attention_gain,
    attention_shift,
    packed_weight,
    packed_bias,
    output_weight,
    output_bias,
    feedforward_gain,
    feedforward_shift,
    expand_weight,
    expand_bias,
    shrink_weight,
    shrink_bias,
    grad_output,
):
    token_count = block_input.shape[0]
    local_width = packed_weight.shape[2]
    local_heads = local_width // HEAD
    score_scale = HEAD ** (-0.5)
    contract_rows = (((0,), (0,)), ((), ()))
    contract_cols = (((1,), (1,)), ((), ()))
    residual = block_input.astype(jnp.float32)
    normed_a, inv_std_a = norm_rows(residual)
    attend_in = (normed_a * attention_gain + attention_shift).astype(jnp.bfloat16)
    cosine, sine_part = rotary_tables(sequence_ids, HEAD)
    same_sequence = (sequence_ids[:, None] == sequence_ids[None, :])[None]
    packed = (
        jnp.einsum("td,dcw->tcw", attend_in, packed_weight, preferred_element_type=jnp.float32)
        + packed_bias
    )
    split_heads = packed.reshape(token_count, 3, local_heads, HEAD)
    queries = rotate(split_heads[:, 0], cosine, sine_part).astype(jnp.bfloat16)
    keys_rot = rotate(split_heads[:, 1], cosine, sine_part).astype(jnp.bfloat16)
    values_low = split_heads[:, 2].astype(jnp.bfloat16)
    scores = (
        jnp.einsum("qhd,khd->hqk", queries, keys_rot, preferred_element_type=jnp.float32)
        * score_scale
    )
    scores = jnp.where(same_sequence, scores, MASKED)
    row_max = jnp.max(scores, axis=-1, keepdims=True)
    log_total = row_max + jnp.log(jnp.sum(jnp.exp(scores - row_max), axis=-1, keepdims=True))
    prob_full = jnp.exp(scores - log_total)
    prob_low = prob_full.astype(jnp.bfloat16)
    attended = jnp.einsum("hqk,khd->qhd", prob_low, values_low, preferred_element_type=jnp.float32)
    attended = attended.reshape(token_count, local_width).astype(jnp.bfloat16)
    mixed = lax.psum(jnp.dot(attended, output_weight, preferred_element_type=jnp.float32), "tensor")
    middle = residual + mixed + output_bias
    normed_b, inv_std_b = norm_rows(middle)
    expand_in = (normed_b * feedforward_gain + feedforward_shift).astype(jnp.bfloat16)
    pre_act = jnp.dot(expand_in, expand_weight, preferred_element_type=jnp.float32) + expand_bias
    activated, gelu_pull = jax.vjp(lambda inner: jax.nn.gelu(inner, approximate=False), pre_act)
    act_low = activated.astype(jnp.bfloat16)
    shrunk = lax.psum(jnp.dot(act_low, shrink_weight, preferred_element_type=jnp.float32), "tensor")
    block_output = (middle + shrunk + shrink_bias).astype(jnp.bfloat16)
    top_grad = grad_output.astype(jnp.float32)
    grad_shrink_bias = jnp.sum(top_grad, axis=0)
    grad_shrink_weight = lax.dot_general(
        act_low, grad_output, contract_rows, preferred_element_type=jnp.float32
    )
    grad_act = lax.dot_general(
        grad_output, shrink_weight, contract_cols, preferred_element_type=jnp.float32
    )
    grad_pre = gelu_pull(grad_act)[0].astype(jnp.bfloat16)
    grad_expand_bias = jnp.sum(grad_pre.astype(jnp.float32), axis=0)
    grad_expand_weight = lax.dot_general(
        expand_in, grad_pre, contract_rows, preferred_element_type=jnp.float32
    )
    grad_expand_in = lax.psum(
        lax.dot_general(grad_pre, expand_weight, contract_cols, preferred_element_type=jnp.float32),
        "tensor",
    )
    grad_feedforward_gain = jnp.sum(grad_expand_in * normed_b, axis=0)
    grad_feedforward_shift = jnp.sum(grad_expand_in, axis=0)
    grad_middle = top_grad + norm_back(grad_expand_in, normed_b, inv_std_b, feedforward_gain)
    grad_output_bias = jnp.sum(grad_middle, axis=0)
    grad_mixed = grad_middle.astype(jnp.bfloat16)
    grad_output_weight = lax.dot_general(
        attended, grad_mixed, contract_rows, preferred_element_type=jnp.float32
    )
    grad_attended = lax.dot_general(
        grad_mixed, output_weight, contract_cols, preferred_element_type=jnp.float32
    )
    grad_attended = grad_attended.astype(jnp.bfloat16).reshape(token_count, local_heads, HEAD)
    grad_probs = jnp.einsum(
        "qhd,khd->hqk", grad_attended, values_low, preferred_element_type=jnp.float32
    )
    row_inner = jnp.sum(prob_full * grad_probs, axis=-1, keepdims=True)
    grad_scores = (prob_full * (grad_probs - row_inner)).astype(jnp.bfloat16)
    grad_values = jnp.einsum(
        "hqk,qhd->khd", prob_low, grad_attended, preferred_element_type=jnp.float32
    )
    grad_queries = (
        jnp.einsum("hqk,khd->qhd", grad_scores, keys_rot, preferred_element_type=jnp.float32)
        * score_scale
    )
    grad_keys = (
        jnp.einsum("hqk,qhd->khd", grad_scores, queries, preferred_element_type=jnp.float32)
        * score_scale
    )
    grad_packed = jnp.stack(
        [
            rotate_back(grad_queries, cosine, sine_part),
            rotate_back(grad_keys, cosine, sine_part),
            grad_values,
        ],
        axis=1,
    )
    grad_packed = grad_packed.reshape(token_count, 3, local_width).astype(jnp.bfloat16)
    grad_packed_bias = jnp.sum(grad_packed.astype(jnp.float32), axis=0)
    grad_packed_weight = jnp.einsum(
        "td,tcw->dcw", attend_in, grad_packed, preferred_element_type=jnp.float32
    )
    grad_attend_in = lax.psum(
        jnp.einsum("tcw,dcw->td", grad_packed, packed_weight, preferred_element_type=jnp.float32),
        "tensor",
    )
    grad_attention_gain = jnp.sum(grad_attend_in * normed_a, axis=0)
    grad_attention_shift = jnp.sum(grad_attend_in, axis=0)
    grad_input = (
        grad_middle + norm_back(grad_attend_in, normed_a, inv_std_a, attention_gain)
    ).astype(jnp.bfloat16)
    width = block_input.shape[1]
    hidden = expand_weight.shape[1]
    small = [
        grad_attention_gain,
        grad_attention_shift,
        grad_packed_bias.reshape(-1),
        grad_output_bias,
        grad_feedforward_gain,
        grad_feedforward_shift,
        grad_expand_bias,
        grad_shrink_bias,
    ]
    sizes = [a.size for a in small]
    flat = jnp.concatenate(small)
    flat = jnp.pad(flat, (0, R * width - flat.size)).reshape(R, width)
    shrink_sum, expand_sum, output_sum, packed_sum, flat = sum_grads(
        n_dp,
        [
            grad_shrink_weight,
            grad_expand_weight,
            grad_output_weight,
            jnp.transpose(grad_packed_weight, (1, 0, 2)),
            flat,
        ],
        width,
        hidden,
        local_width,
    )
    flat = flat.reshape(-1)
    parts = []
    place = 0
    for size in sizes:
        parts.append(flat[place : place + size])
        place += size
    return (
        block_output,
        grad_input,
        parts[0],
        parts[1],
        jnp.transpose(packed_sum, (1, 0, 2)),
        parts[2].reshape(3, local_width),
        output_sum,
        parts[3],
        parts[4],
        parts[5],
        expand_sum,
        parts[6],
        shrink_sum,
        parts[7],
    )


def solution(mesh):
    in_specs = (
        P("dp", None),
        P("dp"),
        P(),
        P(),
        P(None, None, "tensor"),
        P(None, "tensor"),
        P("tensor", None),
        P(),
        P(),
        P(),
        P(None, "tensor"),
        P("tensor"),
        P("tensor", None),
        P(),
        P("dp", None),
    )
    out_specs = (
        P("dp", None),
        P("dp", None),
        P(),
        P(),
        P(None, None, "tensor"),
        P(None, "tensor"),
        P("tensor", None),
        P(),
        P(),
        P(),
        P(None, "tensor"),
        P("tensor"),
        P("tensor", None),
        P(),
    )
    return jax.shard_map(
        functools.partial(body, mesh.shape["dp"]), mesh=mesh, in_specs=in_specs, out_specs=out_specs, check_vma=False)
```

```python
import functools
import math

import jax
import jax.numpy as jnp
import numpy as np
from jax import lax
from jax.experimental import pallas as pl
from jax.experimental.pallas import tpu as pltpu
from jax.sharding import PartitionSpec as P

HEAD = 64
EPSILON = 1e-05
MASKED = -1000000000.0
LANES = 128
MESH = pl.DeviceIdType.MESH
W = 8
R = 64
LF = 2


class Comm:
    def __init__(self, n, counts, G, O, RF, RU, RD, RL, sems):
        self.nz = n // 4
        self.counts = counts
        self.G, self.O, self.RF, self.RU, self.RD, self.RL = G, O, RF, RU, RD, RL
        self.sems = sems
        d = lax.axis_index("dp")
        self.t = lax.axis_index("tensor")
        self.d = d
        self.z = d // 4
        self.y = (d // 2) % 2
        self.x = d % 2
        self.px = d + 1 - 2 * self.x
        self.py = d + 2 - 4 * self.y

    def steps(self):
        return max(self.counts) + LF + 2 * self.nz + 3

    def barrier(self):
        b = pltpu.get_barrier_semaphore()
        for peer in ((self.px, self.t), (self.py, self.t), (self.d, 1 - self.t)):
            pl.semaphore_signal(b, inc=1, device_id=peer, device_id_type=MESH)

        @pl.when(self.z > 0)
        def _():
            pl.semaphore_signal(b, inc=1, device_id=(self.d - 4, self.t), device_id_type=MESH)

        @pl.when(self.z < self.nz - 1)
        def _():
            pl.semaphore_signal(b, inc=1, device_id=(self.d + 4, self.t), device_id_type=MESH)

        edge = (self.z > 0).astype(jnp.int32) + (self.z < self.nz - 1).astype(jnp.int32)
        pl.semaphore_wait(b, 3 + edge)

    def rows(self, start, size):
        return self.G.at[pl.ds(pl.multiple_of(start, 8), size), :]

    def done(self, start, size):
        return self.O.at[pl.ds(pl.multiple_of(start, 8), size), :]

    def copy(self, src, dst, kind, idx, dev):
        return pltpu.make_async_remote_copy(
            src_ref=src, dst_ref=dst, send_sem=self.sems[kind + "s"].at[idx], recv_sem=self.sems[kind + "r"].at[idx],
            device_id=(dev, self.t), device_id_type=MESH)

    def add(self, start, size, buf):
        r = self.rows(start, size)
        r[...] = r[...] + buf[...]

    def step(self, i):
        for c in (0, 1):
            self.first(c, i)
        for c in (0, 1):
            self.rest(c, i)

    def base(self, c, k):
        return (2 * k + c) * R

    def f_copy(self, c, k):
        a, dev = (self.x, self.px) if c == 0 else (self.y, self.py)
        q = k % W
        return self.copy(self.rows(self.base(c, k) + (1 - a) * (R // 2), R // 2), self.RF.at[c, q], "F", (c, q), dev)

    def first(self, c, i):
        @pl.when(i < self.counts[c])
        def _():
            self.f_copy(c, i).start()

    def rest(self, c, i):
        nz, z = self.nz, self.z
        a, fdev, b, ldev = (self.x, self.px, self.y, self.py) if c == 0 else (self.y, self.py, self.x, self.px)
        n = self.counts[c]
        H, Q, E = R // 2, R // 4, R // 8

        def ok(k):
            return (k >= 0) & (k < n)

        def half(k):
            return self.base(c, k) + a * H

        def sub(k, s):
            return half(k) + s * Q

        def root(k, s):
            return k % 2 if s == 0 else nz - 1 - k % 2

        k = i - LF

        @pl.when(ok(k))
        def _(k=k):
            cp = self.f_copy(c, k)
            cp.wait_send()
            cp.wait_recv()
            self.add(half(k), H, self.RF.at[c, k % W])

        def up(k, s):
            return self.copy(self.rows(sub(k, s), Q), self.RU.at[c, s, k % W], "U", (c, s, k % W), jnp.minimum(self.d + 4, 4 * nz - 1))

        def dn(k, s):
            return self.copy(self.rows(sub(k, s), Q), self.RD.at[c, s, k % W], "D", (c, s, k % W), jnp.maximum(self.d - 4, 0))

        for s in (0, 1):
            k = i - (LF + z)

            @pl.when(ok(k) & (z <= root(k, s)) & (z > 0))
            def _(k=k, s=s):
                up(k, s).wait_recv()
                self.add(sub(k, s), Q, self.RU.at[c, s, k % W])

            @pl.when(ok(k) & (z < root(k, s)))
            def _(k=k, s=s):
                up(k, s).start()

            k = i - (LF + nz - 1 - z)

            @pl.when(ok(k) & (z >= root(k, s)) & (z < nz - 1))
            def _(k=k, s=s):
                dn(k, s).wait_recv()
                self.add(sub(k, s), Q, self.RD.at[c, s, k % W])

            @pl.when(ok(k) & (z > root(k, s)))
            def _(k=k, s=s):
                dn(k, s).start()

            k = i - (LF + z + 1)

            @pl.when(ok(k) & (z < root(k, s)))
            def _(k=k, s=s):
                up(k, s).wait_send()

            k = i - (LF + nz - 1 - z + 1)

            @pl.when(ok(k) & (z > root(k, s)))
            def _(k=k, s=s):
                dn(k, s).wait_send()

        def last(k, s):
            return self.copy(self.rows(sub(k, s) + (1 - b) * E, E), self.RL.at[c, k % W], "L", (c, k % W), ldev)

        def last_back(k, s):
            at = sub(k, s) + b * E
            return self.copy(self.rows(at, E), self.done(at, E), "M", (c, k % W), ldev)

        for s in (0, 1):
            k = i - (LF + nz - 1)

            @pl.when(ok(k) & (z == root(k, s)))
            def _(k=k, s=s):
                last(k, s).start()

            k = i - (LF + nz)

            @pl.when(ok(k) & (z == root(k, s)))
            def _(k=k, s=s):
                cp = last(k, s)
                cp.wait_send()
                cp.wait_recv()
                self.add(sub(k, s) + b * E, E, self.RL.at[c, k % W])
                last_back(k, s).start()
                self.done(sub(k, s) + b * E, E)[...] = self.rows(sub(k, s) + b * E, E)[...]

        def g_up(k, s):
            r = self.done(sub(k, s), Q)
            return self.copy(r, r, "V", (c, s, k % W), jnp.minimum(self.d + 4, 4 * nz - 1))

        def g_dn(k, s):
            r = self.done(sub(k, s), Q)
            return self.copy(r, r, "E", (c, s, k % W), jnp.maximum(self.d - 4, 0))

        def g_first(k, s):
            r = self.done(sub(k, s), Q)
            return self.copy(r, r, "G", (c, s, k % W), fdev)

        for e in (0, 1):
            for s in (0, 1):
                r = e if s == 0 else nz - 1 - e
                lag = LF + nz + 1 + jnp.abs(z - r)
                k = i - lag
                here = ok(k) & (k % 2 == e)

                @pl.when(here & (z == r))
                def _(k=k, s=s):
                    cp = last_back(k, s)
                    cp.wait_send()
                    cp.wait_recv()

                @pl.when(here & (z < r))
                def _(k=k, s=s):
                    g_dn(k, s).wait_recv()

                @pl.when(here & (z > r))
                def _(k=k, s=s):
                    g_up(k, s).wait_recv()

                @pl.when(here & (z <= r) & (z > 0))
                def _(k=k, s=s):
                    g_dn(k, s).start()

                @pl.when(here & (z >= r) & (z < nz - 1))
                def _(k=k, s=s):
                    g_up(k, s).start()

                @pl.when(here)
                def _(k=k, s=s):
                    g_first(k, s).start()

                k = i - (lag + 1)
                here = ok(k) & (k % 2 == e)

                @pl.when(here)
                def _(k=k, s=s):
                    cp = g_first(k, s)
                    cp.wait_send()
                    cp.wait_recv()

                @pl.when(here & (z <= r) & (z > 0))
                def _(k=k, s=s):
                    g_dn(k, s).wait_send()

                @pl.when(here & (z >= r) & (z < nz - 1))
                def _(k=k, s=s):
                    g_up(k, s).wait_send()


KINDS = {"F": (2, W), "U": (2, 2, W), "D": (2, 2, W), "L": (2, W), "M": (2, W), "V": (2, 2, W), "E": (2, 2, W), "G": (2, 2, W)}
SEMS = [k + e for k in KINDS for e in "sr"]


def comm_scratch(width):
    return [
        pltpu.VMEM((2, W, R // 2, width), jnp.float32),
        pltpu.VMEM((2, 2, W, R // 4, width), jnp.float32),
        pltpu.VMEM((2, 2, W, R // 4, width), jnp.float32),
        pltpu.VMEM((2, W, R // 8, width), jnp.float32),
    ] + [pltpu.SemaphoreType.DMA(KINDS[k[0]]) for k in SEMS]

def f32dot(a, b, dims=((1,), (0,))):
    return lax.dot_general(a, b, (dims, ((), ())), preferred_element_type=jnp.float32)


NT = ((1,), (1,))
TN = ((0,), (0,))


def tables(tokens):
    half = HEAD // 2
    frequency = np.exp(np.arange(half) * (-2.0 * math.log(10000.0) / HEAD)).astype(np.float32)
    angles = (np.arange(tokens, dtype=np.float32)[:, None] * frequency[None, :]).astype(np.float64)
    cosine = np.tile(np.cos(angles), (1, LANES // half)).astype(np.float32)
    sign = np.where((np.arange(LANES) // half) % 2 == 0, -1.0, 1.0)
    sine = (np.tile(np.sin(angles), (1, LANES // half)) * sign).astype(np.float32)
    return cosine, sine


def swap_halves(v, low):
    return jnp.where(low, pltpu.roll(v, LANES - HEAD // 2, 1), pltpu.roll(v, HEAD // 2, 1))


def chunks(total, size, body, unroll=False):
    count = total // size

    def one(i, carry):
        body(pl.multiple_of(i * size, size))
        return carry

    lax.fori_loop(0, count, one, 0, unroll=unroll)


def mean_of(v):
    return jnp.mean(v, axis=-1, keepdims=True)


def norm(v):
    centred = v - mean_of(v)
    inv = lax.rsqrt(mean_of(centred * centred) + EPSILON)
    return centred * inv, inv


class Row:
    def __init__(self, ref):
        self.ref = ref

    def __getitem__(self, index):
        v = self.ref[...] if index is Ellipsis else self.ref[index[1]]
        return v.reshape(1, v.shape[0])


def layer_kernel(n, *refs):
    (x_h, ids, ag_h, as_h, wp_h, pb_h, wo_h, ob_h, fg_h, fs_h, we_h, eb_h, ws_h, sb_h, go_h, cos_h, sin_h) = refs[:17]
    O, bo, gi = refs[17:20]
    (x, ag, ash, wp, pb, wo, ob, fg, fs, we, eb, ws, sb, go, cos, sin) = refs[20:36]
    ag, ash, ob, fg, fs, eb, sb = (Row(v) for v in (ag, ash, ob, fg, fs, eb, sb))
    (ain, qkv, att, prob, mid, ein, act, PX, RX, dqkv, G, RF, RU, RD, RL, local, xs, xr) = refs[36:54]
    sems = dict(zip(SEMS, refs[54:]))
    T, D = x.shape
    WL = wo.shape[0]
    FL = ws.shape[0]
    half = T // 2
    parts = WL // LANES
    base_out, base_pack = FL + D * (FL // D), FL + D * (FL // D) + WL
    base_small = base_pack + D + WL
    full = base_small // (2 * R)
    comm = Comm(n, (full + 1, full), G, O, RF, RU, RD, RL, sems)

    loads = []
    for j, (src, dst) in enumerate(
        [(x_h, x), (wp_h, wp), (cos_h, cos), (sin_h, sin), (ag_h, ag.ref), (as_h, ash.ref), (pb_h, pb), (wo_h, wo), (ob_h, ob.ref), (fg_h, fg.ref), (fs_h, fs.ref), (we_h, we), (eb_h, eb.ref), (go_h, go), (ws_h, ws), (sb_h, sb.ref)]
    ):
        cp = pltpu.make_async_copy(src, dst, local.at[j])
        cp.start()
        loads.append(cp)
    comm.barrier()
    for j in (0, 4, 5):
        loads[j].wait()

    lane = lax.broadcasted_iota(jnp.int32, (1, LANES), 1)
    low_half = (lane // (HEAD // 2)) % 2 == 0
    first_head = lane < HEAD
    other = (ids[T - 1] > 0).astype(jnp.float32)
    col = lax.broadcasted_iota(jnp.int32, (1, T), 1)
    top_bias = jnp.where(col < half, 0.0, MASKED * other)
    low_bias = jnp.where(col < half, MASKED * other, 0.0)

    for j in (2, 3):
        loads[j].wait()
    for table in (cos, sin):
        table[pl.ds(half, half), :] = table[pl.ds(half, half), :] * (1.0 - other) + table[pl.ds(0, half), :] * other

    def pre_part(p):
        return G.at[pl.ds(base_pack + p * T, T), :]

    def norm_in(r):
        rows = pl.ds(r, 64)
        normed, _ = norm(x[rows, :].astype(jnp.float32))
        ain[rows, :] = (normed * ag[...] + ash[...]).astype(jnp.bfloat16)

    chunks(T, 64, norm_in)
    for j in (1, 6):
        loads[j].wait()
    tmp = PX.at[0]
    for c in range(3):
        tmp[:, pl.ds(0, WL)] = f32dot(ain[...], wp[c])

        def turn(r, c=c):
            rows = pl.ds(r, 64)
            for j in range(parts):
                v = tmp[rows, pl.ds(j * LANES, LANES)] + pb[pl.ds(c, 1), pl.ds(j * LANES, LANES)]
                if c < 2:
                    v = v * cos[rows, :] + swap_halves(v, low_half) * sin[rows, :]
                if c == 0:
                    v = v.astype(jnp.bfloat16) * jnp.bfloat16(HEAD**-0.5)
                qkv[c * parts + j, rows, :] = v.astype(jnp.bfloat16)

        chunks(T, 64, turn)

    QR = 128

    def attend(j, carry):
        keys, vals = qkv[parts + j], qkv[2 * parts + j]
        for r in range(0, T, QR):
            q = qkv[j, r : r + QR, :]
            bias = top_bias if r < half else low_bias
            outs = []
            for e in (0, 1):
                qm = jnp.where(first_head if e == 0 else ~first_head, q, jnp.zeros_like(q))
                s = f32dot(qm, keys, NT) + bias
                p = jnp.exp(s - jnp.max(s, axis=-1, keepdims=True))
                p = (p * (1.0 / jnp.sum(p, axis=-1, keepdims=True))).astype(jnp.bfloat16)
                prob[2 * j + e, r : r + QR, :] = p
                outs.append(f32dot(p, vals))
            att[r : r + QR, pl.ds(pl.multiple_of(j * LANES, LANES), LANES)] = jnp.where(first_head, *outs).astype(jnp.bfloat16)
        return carry

    lax.fori_loop(0, parts, attend, 0)

    def swap(i, h):
        rows = pl.ds(h * half, half)
        return pltpu.make_async_remote_copy(
            src_ref=PX.at[i % 2, rows, :], dst_ref=RX.at[i % 2, rows, :], send_sem=xs.at[i, h], recv_sem=xr.at[i, h],
            device_id=(comm.d, 1 - comm.t), device_id_type=MESH)

    for j in (7, 8, 9, 10):
        loads[j].wait()
    for h in (0, 1):
        rows = pl.ds(h * half, half)
        PX[0, rows, :] = f32dot(att[rows, :], wo[...])
        swap(0, h).start()
    for h in (0, 1):
        swap(0, h).wait_recv()

        def middle_rows(r, h=h):
            rows = pl.ds(h * half + r, 64)
            v = x[rows, :].astype(jnp.float32) + (PX[0, rows, :] + RX[0, rows, :]) + ob[...]
            mid[rows, :] = v
            normed, _ = norm(v)
            ein[rows, :] = (normed * fg[...] + fs[...]).astype(jnp.bfloat16)

        chunks(half, 64, middle_rows)
    for j in (11, 12):
        loads[j].wait()

    NB = WL
    per = D // NB

    for b in range(FL // NB):
        cols = pl.ds(b * NB, NB)
        here = pl.ds((b % per) * NB, NB)
        pre = pre_part(b // per)
        pre[:, here] = f32dot(ein[...], we[:, cols])

        def gelu_rows(r, pre=pre, here=here, cols=cols):
            rows = pl.ds(r, 64)
            v = pre[rows, here] + eb[:, cols]
            pre[rows, here] = v
            act[rows, cols] = (v * (0.5 + 0.5 * lax.erf(v * math.sqrt(0.5)))).astype(jnp.bfloat16)

        chunks(T, 64, gelu_rows)
    loads[13].wait()
    for b in range(FL // NB):
        G[pl.ds(b * NB, NB), :] = f32dot(act[:, pl.ds(b * NB, NB)], go[...], TN)
    swap(0, 0).wait_send()
    swap(0, 1).wait_send()
    for j in (14, 15):
        loads[j].wait()

    for h in (0, 1):
        rows = pl.ds(h * half, half)
        PX[1, rows, :] = f32dot(act[rows, :], ws[...])
        swap(1, h).start()
    for h in (0, 1):
        swap(1, h).wait()

        def out_rows(r, h=h):
            rows = pl.ds(h * half + r, 64)
            bo[rows, :] = (mid[rows, :] + (PX[1, rows, :] + RX[1, rows, :]) + sb[...]).astype(jnp.bfloat16)

        chunks(half, 64, out_rows)

    def small_row(k):
        return G.at[pl.ds(base_small + k, 1), :]

    for b in range(FL // NB):
        cols = pl.ds(b * NB, NB)
        here = pl.ds((b % per) * NB, NB)
        pre = pre_part(b // per)
        PX[0, :, pl.ds(0, NB)] = f32dot(go[...], ws[cols, :], NT)

        def slope_rows(i, total, pre=pre, here=here, cols=cols):
            rows = pl.ds(pl.multiple_of(i * 64, 64), 64)
            v = pre[rows, here]
            slope = 0.5 + 0.5 * lax.erf(v * math.sqrt(0.5)) + v * (jnp.exp(v * v * -0.5) * (1.0 / math.sqrt(2.0 * math.pi)))
            g = (PX[0, rows, pl.ds(0, NB)] * slope).astype(jnp.bfloat16)
            act[rows, cols] = g
            return total + jnp.sum(g.astype(jnp.float32), axis=0, keepdims=True)

        total = lax.fori_loop(0, T // 64, slope_rows, jnp.zeros((1, NB), jnp.float32))
        G[pl.ds(base_small + 6 + b // per, 1), here] = total
    for p in range(FL // D):
        for b in range(D // NB):
            G[pl.ds(FL + p * D + b * NB, NB), :] = f32dot(ein[:, pl.ds(b * NB, NB)], act[:, pl.ds(p * D, D)], TN)

    for h in (0, 1):
        rows = pl.ds(h * half, half)
        PX[0, rows, :] = f32dot(act[rows, :], we[...], NT)
        swap(2, h).start()

    zero = jnp.zeros((1, D), jnp.float32)
    sums = (zero, zero, zero, zero)
    for h in (0, 1):
        swap(2, h).wait()

        def back_rows(i, totals, h=h):
            rows = pl.ds(pl.multiple_of(h * half + i * 32, 32), 32)
            gain_sum, shift_sum, bias_sum, top_sum = totals
            g = PX[0, rows, :] + RX[0, rows, :]
            normed, inv = norm(mid[rows, :])
            scaled = g * fg[...]
            top = go[rows, :].astype(jnp.float32)
            gm = top + (scaled - mean_of(scaled) - normed * mean_of(scaled * normed)) * inv
            mid[rows, :] = gm
            ein[rows, :] = gm.astype(jnp.bfloat16)
            return (
                gain_sum + jnp.sum(g * normed, axis=0, keepdims=True),
                shift_sum + jnp.sum(g, axis=0, keepdims=True),
                bias_sum + jnp.sum(gm, axis=0, keepdims=True),
                top_sum + jnp.sum(top, axis=0, keepdims=True),
            )

        sums = lax.fori_loop(0, half // 32, back_rows, sums)
    for k, v in zip((3, 4, 2, 5), sums):
        small_row(k)[...] = v

    G[pl.ds(base_out, WL), :] = f32dot(att[...], ein[...], TN)
    att[...] = f32dot(ein[...], wo[...], NT).astype(jnp.bfloat16)

    def attend_back(j, carry):
        keys, vals, queries = qkv[parts + j], qkv[2 * parts + j], qkv[j]
        at = pl.ds(pl.multiple_of(j * LANES, LANES), LANES)
        dv = [None, None]
        dk = [None, None]
        for r in range(0, T, QR):
            rows = pl.ds(r, QR)
            do = att[rows, at]
            q = qkv[j, rows, :]
            dq = []
            for e in (0, 1):
                dom = jnp.where(first_head if e == 0 else ~first_head, do, jnp.zeros_like(do))
                p_low = prob[2 * j + e, rows, :]
                p = p_low.astype(jnp.float32)
                dp = f32dot(dom, vals, NT)
                inner = jnp.sum(p * dp, axis=-1, keepdims=True)
                ds = (p * (dp - inner)).astype(jnp.bfloat16)
                dq.append(f32dot(ds, keys))
                add_v = f32dot(p_low, do, TN)
                add_k = f32dot(ds, q, TN)
                dv[e] = add_v if r == 0 else dv[e] + add_v
                dk[e] = add_k if r == 0 else dk[e] + add_k
            v = jnp.where(first_head, *dq) * (HEAD**-0.5)
            dqkv[j, rows, :] = (v * cos[rows, :] - swap_halves(v, low_half) * sin[rows, :]).astype(jnp.bfloat16)
        dqkv[2 * parts + j] = jnp.where(first_head, *dv).astype(jnp.bfloat16)
        v = jnp.where(first_head, *dk)
        dqkv[parts + j] = (v * cos[...] - swap_halves(v, low_half) * sin[...]).astype(jnp.bfloat16)
        return carry

    lax.fori_loop(0, parts, attend_back, 0)

    for c in range(3):
        for j in range(parts):
            g = dqkv[c * parts + j]
            cols = pl.ds(j * LANES, LANES)
            G[pl.ds(base_small + 8 + c, 1), cols] = jnp.sum(g.astype(jnp.float32), axis=0, keepdims=True)
            grad = f32dot(ain[...], g, TN)
            if c < 2:
                G[pl.ds(base_pack, D), pl.ds(c * WL + j * LANES, LANES)] = grad
            else:
                for p in range(2):
                    G[pl.ds(base_pack + D, WL), pl.ds(p * WL + j * LANES, LANES)] = grad[p * WL : (p + 1) * WL, :]

    for h in (0, 1):
        rows = pl.ds(h * half, half)
        acc = None
        for c in range(3):
            for j in range(parts):
                term = f32dot(dqkv[c * parts + j, rows, :], wp[c, :, pl.ds(j * LANES, LANES)], NT)
                acc = term if acc is None else acc + term
        PX[1, rows, :] = acc
        swap(3, h).start()
    sums = (zero, zero)
    for h in (0, 1):
        swap(3, h).wait()

        def input_rows(i, totals, h=h):
            rows = pl.ds(pl.multiple_of(h * half + i * 32, 32), 32)
            g = PX[1, rows, :] + RX[1, rows, :]
            normed, inv = norm(x[rows, :].astype(jnp.float32))
            scaled = g * ag[...]
            v = mid[rows, :] + (scaled - mean_of(scaled) - normed * mean_of(scaled * normed)) * inv
            gi[rows, :] = v.astype(jnp.bfloat16)
            return (
                totals[0] + jnp.sum(g * normed, axis=0, keepdims=True),
                totals[1] + jnp.sum(g, axis=0, keepdims=True),
            )

        sums = lax.fori_loop(0, half // 32, input_rows, sums)
    small_row(0)[...] = sums[0]
    small_row(1)[...] = sums[1]
    G[pl.ds(base_small + 8, 3), pl.ds(WL, D - WL)] = jnp.zeros((3, D - WL), jnp.float32)
    G[pl.ds(base_small + 11, R - 11), :] = jnp.zeros((R - 11, D), jnp.float32)

    def body(i, carry):
        comm.step(i)
        return carry

    lax.fori_loop(0, comm.steps(), body, 0)


def unpack(moves_of, whole_ref, bo_ref, gi_ref, *refs):
    outs, local = refs[:-1], refs[-1]
    stores = []
    pairs, rows = moves_of(whole_ref, bo_ref, gi_ref, outs)
    for pair in pairs:
        cp = pltpu.make_async_copy(*pair, local.at[len(stores)])
        cp.start()
        stores.append(cp)
    for src, dst in rows:
        dst[...] = src[...]
    for cp in stores:
        cp.wait()


def unpack_moves(T, D, WL, FL, O, bo, gi, outs):
    base_out = FL + D * (FL // D)
    base_pack = base_out + WL
    base_small = base_pack + D + WL
    pairs = [(bo, outs[0]), (gi, outs[1]), (O.at[pl.ds(0, FL), :], outs[2])]
    for p in range(FL // D):
        pairs.append((O.at[pl.ds(FL + p * D, D), :], outs[3].at[:, pl.ds(p * D, D)]))
    pairs.append((O.at[pl.ds(base_out, WL), :], outs[4]))
    for c in range(2):
        pairs.append((O.at[pl.ds(base_pack, D), pl.ds(c * WL, WL)], outs[5].at[c]))
    for p in range(2):
        pairs.append((O.at[pl.ds(base_pack + D, WL), pl.ds(p * WL, WL)], outs[5].at[2, pl.ds(p * WL, WL), :]))
    rows = [(O.at[base_small + k, :], outs[6 + k]) for k in range(6)]
    for p in range(FL // D):
        rows.append((O.at[base_small + 6 + p, :], outs[12].at[pl.ds(p * D, D)]))
    rows.append((O.at[pl.ds(base_small + 8, 3), pl.ds(0, WL)], outs[13]))
    return pairs, rows


def body(
    n_dp,
    block_input,
    sequence_ids,
    attention_gain,
    attention_shift,
    packed_weight,
    packed_bias,
    output_weight,
    output_bias,
    feedforward_gain,
    feedforward_shift,
    expand_weight,
    expand_bias,
    shrink_weight,
    shrink_bias,
    grad_output,
):
    T, D = block_input.shape
    WL = packed_weight.shape[2]
    FL = shrink_weight.shape[0]
    parts = WL // LANES
    bf16, f32 = jnp.bfloat16, jnp.float32
    cosine, sine = tables(T)
    total = FL + D * (FL // D) + WL + D + WL + R

    args = [
        block_input,
        sequence_ids,
        attention_gain,
        attention_shift,
        jnp.transpose(packed_weight, (1, 0, 2)),
        packed_bias,
        output_weight,
        output_bias,
        feedforward_gain,
        feedforward_shift,
        expand_weight,
        expand_bias,
        shrink_weight,
        shrink_bias,
        grad_output,
        jnp.asarray(cosine),
        jnp.asarray(sine),
    ]
    hbm = pl.BlockSpec(memory_space=pltpu.HBM)
    vmem = pl.BlockSpec(memory_space=pltpu.VMEM)
    held = [pltpu.VMEM(a.shape, a.dtype) for i, a in enumerate(args) if i != 1]
    scratch = comm_scratch(D)
    whole, out, grad_in = pl.pallas_call(
        functools.partial(layer_kernel, n_dp),
        out_shape=[pltpu.VMEM((total, D), f32), pltpu.VMEM((T, D), bf16), pltpu.VMEM((T, D), bf16)],
        in_specs=[hbm, pl.BlockSpec(memory_space=pltpu.SMEM)] + [hbm] * 15,
        out_specs=[vmem] * 3,
        scratch_shapes=held
        + [
            pltpu.VMEM((T, D), bf16),
            pltpu.VMEM((3 * parts, T, LANES), bf16),
            pltpu.VMEM((T, WL), bf16),
            pltpu.VMEM((2 * parts, T, T), bf16),
            pltpu.VMEM((T, D), f32),
            pltpu.VMEM((T, D), bf16),
            pltpu.VMEM((T, FL), bf16),
            pltpu.VMEM((2, T, D), f32),
            pltpu.VMEM((2, T, D), f32),
            pltpu.VMEM((3 * parts, T, LANES), bf16),
            pltpu.VMEM((total, D), f32),
        ]
        + scratch[:4]
        + [pltpu.SemaphoreType.DMA((16,)), pltpu.SemaphoreType.DMA((4, 2)), pltpu.SemaphoreType.DMA((4, 2))]
        + scratch[4:],
        compiler_params=pltpu.CompilerParams(
            collective_id=0, has_side_effects=True, vmem_limit_bytes=48 << 20
        ),
    )(*args)
    shapes = [
        ((T, D), bf16),
        ((T, D), bf16),
        ((FL, D), f32),
        ((D, FL), f32),
        ((WL, D), f32),
        ((3, D, WL), f32),
        *[((D,), f32)] * 6,
        ((FL,), f32),
        ((3, WL), f32),
    ]
    anywhere = pl.BlockSpec(memory_space=pl.ANY)
    got = pl.pallas_call(
        functools.partial(unpack, functools.partial(unpack_moves, T, D, WL, FL)),
        out_shape=[pltpu.HBM(*s) for s in shapes[:6]] + [jax.ShapeDtypeStruct(*s) for s in shapes[6:]],
        in_specs=[vmem] * 3,
        out_specs=[anywhere] * 6 + [vmem] * 8,
        scratch_shapes=[pltpu.SemaphoreType.DMA((32,))],
        compiler_params=pltpu.CompilerParams(vmem_limit_bytes=1 << 20),
    )(whole, out, grad_in)
    small = got[6:12]
    return (
        got[0],
        got[1],
        small[0],
        small[1],
        jnp.transpose(got[5], (1, 0, 2)),
        got[13],
        got[4],
        small[2],
        small[3],
        small[4],
        got[3],
        got[12],
        got[2],
        small[5],
    )


def solution(mesh):
    in_specs = (
        P("dp", None),
        P("dp"),
        P(),
        P(),
        P(None, None, "tensor"),
        P(None, "tensor"),
        P("tensor", None),
        P(),
        P(),
        P(),
        P(None, "tensor"),
        P("tensor"),
        P("tensor", None),
        P(),
        P("dp", None),
    )
    out_specs = (
        P("dp", None),
        P("dp", None),
        P(),
        P(),
        P(None, None, "tensor"),
        P(None, "tensor"),
        P("tensor", None),
        P(),
        P(),
        P(),
        P(None, "tensor"),
        P("tensor"),
        P("tensor", None),
        P(),
    )
    return jax.shard_map(
        functools.partial(body, mesh.shape["dp"]), mesh=mesh, in_specs=in_specs, out_specs=out_specs, check_vma=False
    )
```

```python
import functools
import math

import jax
import jax.numpy as jnp
import numpy as np
from jax import lax
from jax.experimental import pallas as pl
from jax.experimental.pallas import tpu as pltpu
from jax.sharding import PartitionSpec as P

HEAD = 64
EPSILON = 1e-05
MASKED = -1000000000.0
LANES = 128
MESH = pl.DeviceIdType.MESH
W = 8
R = 64
LF = 2


class Comm:
    def __init__(self, n, counts, G, O, RF, RU, RD, RL, sems):
        self.nz = n // 4
        self.counts = counts
        self.G, self.O, self.RF, self.RU, self.RD, self.RL = G, O, RF, RU, RD, RL
        self.sems = sems
        d = lax.axis_index("dp")
        self.t = lax.axis_index("tensor")
        self.d = d
        self.z = d // 4
        self.y = (d // 2) % 2
        self.x = d % 2
        self.px = d + 1 - 2 * self.x
        self.py = d + 2 - 4 * self.y

    def steps(self):
        return max(self.counts) + LF + 2 * self.nz + 3

    def barrier(self):
        b = pltpu.get_barrier_semaphore()
        for peer in ((self.px, self.t), (self.py, self.t), (self.d, 1 - self.t)):
            pl.semaphore_signal(b, inc=1, device_id=peer, device_id_type=MESH)

        @pl.when(self.z > 0)
        def _():
            pl.semaphore_signal(b, inc=1, device_id=(self.d - 4, self.t), device_id_type=MESH)

        @pl.when(self.z < self.nz - 1)
        def _():
            pl.semaphore_signal(b, inc=1, device_id=(self.d + 4, self.t), device_id_type=MESH)

        edge = (self.z > 0).astype(jnp.int32) + (self.z < self.nz - 1).astype(jnp.int32)
        pl.semaphore_wait(b, 3 + edge)

    def rows(self, start, size):
        return self.G.at[pl.ds(pl.multiple_of(start, 8), size), :]

    def done(self, start, size):
        return self.O.at[pl.ds(pl.multiple_of(start, 8), size), :]

    def copy(self, src, dst, kind, idx, dev):
        return pltpu.make_async_remote_copy(
            src_ref=src, dst_ref=dst, send_sem=self.sems[kind + "s"].at[idx], recv_sem=self.sems[kind + "r"].at[idx],
            device_id=(dev, self.t), device_id_type=MESH)

    def add(self, start, size, buf):
        r = self.rows(start, size)
        r[...] = r[...] + buf[...]

    def step(self, i):
        for c in (0, 1):
            self.first(c, i)
        for c in (0, 1):
            self.rest(c, i)

    def base(self, c, k):
        return (2 * k + c) * R

    def f_copy(self, c, k):
        a, dev = (self.x, self.px) if c == 0 else (self.y, self.py)
        q = k % W
        return self.copy(self.rows(self.base(c, k) + (1 - a) * (R // 2), R // 2), self.RF.at[c, q], "F", (c, q), dev)

    def first(self, c, i):
        @pl.when(i < self.counts[c])
        def _():
            self.f_copy(c, i).start()

    def rest(self, c, i):
        nz, z = self.nz, self.z
        a, fdev, b, ldev = (self.x, self.px, self.y, self.py) if c == 0 else (self.y, self.py, self.x, self.px)
        n = self.counts[c]
        H, Q, E = R // 2, R // 4, R // 8

        def ok(k):
            return (k >= 0) & (k < n)

        def half(k):
            return self.base(c, k) + a * H

        def sub(k, s):
            return half(k) + s * Q

        def root(k, s):
            return k % 2 if s == 0 else nz - 1 - k % 2

        k = i - LF

        @pl.when(ok(k))
        def _(k=k):
            cp = self.f_copy(c, k)
            cp.wait_send()
            cp.wait_recv()
            self.add(half(k), H, self.RF.at[c, k % W])

        def up(k, s):
            return self.copy(self.rows(sub(k, s), Q), self.RU.at[c, s, k % W], "U", (c, s, k % W), jnp.minimum(self.d + 4, 4 * nz - 1))

        def dn(k, s):
            return self.copy(self.rows(sub(k, s), Q), self.RD.at[c, s, k % W], "D", (c, s, k % W), jnp.maximum(self.d - 4, 0))

        for s in (0, 1):
            k = i - (LF + z)

            @pl.when(ok(k) & (z <= root(k, s)) & (z > 0))
            def _(k=k, s=s):
                up(k, s).wait_recv()
                self.add(sub(k, s), Q, self.RU.at[c, s, k % W])

            @pl.when(ok(k) & (z < root(k, s)))
            def _(k=k, s=s):
                up(k, s).start()

            k = i - (LF + nz - 1 - z)

            @pl.when(ok(k) & (z >= root(k, s)) & (z < nz - 1))
            def _(k=k, s=s):
                dn(k, s).wait_recv()
                self.add(sub(k, s), Q, self.RD.at[c, s, k % W])

            @pl.when(ok(k) & (z > root(k, s)))
            def _(k=k, s=s):
                dn(k, s).start()

            k = i - (LF + z + 1)

            @pl.when(ok(k) & (z < root(k, s)))
            def _(k=k, s=s):
                up(k, s).wait_send()

            k = i - (LF + nz - 1 - z + 1)

            @pl.when(ok(k) & (z > root(k, s)))
            def _(k=k, s=s):
                dn(k, s).wait_send()

        def last(k, s):
            return self.copy(self.rows(sub(k, s) + (1 - b) * E, E), self.RL.at[c, k % W], "L", (c, k % W), ldev)

        def last_back(k, s):
            at = sub(k, s) + b * E
            return self.copy(self.rows(at, E), self.done(at, E), "M", (c, k % W), ldev)

        for s in (0, 1):
            k = i - (LF + nz - 1)

            @pl.when(ok(k) & (z == root(k, s)))
            def _(k=k, s=s):
                last(k, s).start()

            k = i - (LF + nz)

            @pl.when(ok(k) & (z == root(k, s)))
            def _(k=k, s=s):
                cp = last(k, s)
                cp.wait_send()
                cp.wait_recv()
                self.add(sub(k, s) + b * E, E, self.RL.at[c, k % W])
                last_back(k, s).start()
                self.done(sub(k, s) + b * E, E)[...] = self.rows(sub(k, s) + b * E, E)[...]

        def g_up(k, s):
            r = self.done(sub(k, s), Q)
            return self.copy(r, r, "V", (c, s, k % W), jnp.minimum(self.d + 4, 4 * nz - 1))

        def g_dn(k, s):
            r = self.done(sub(k, s), Q)
            return self.copy(r, r, "E", (c, s, k % W), jnp.maximum(self.d - 4, 0))

        def g_first(k, s):
            r = self.done(sub(k, s), Q)
            return self.copy(r, r, "G", (c, s, k % W), fdev)

        for e in (0, 1):
            for s in (0, 1):
                r = e if s == 0 else nz - 1 - e
                lag = LF + nz + 1 + jnp.abs(z - r)
                k = i - lag
                here = ok(k) & (k % 2 == e)

                @pl.when(here & (z == r))
                def _(k=k, s=s):
                    cp = last_back(k, s)
                    cp.wait_send()
                    cp.wait_recv()

                @pl.when(here & (z < r))
                def _(k=k, s=s):
                    g_dn(k, s).wait_recv()

                @pl.when(here & (z > r))
                def _(k=k, s=s):
                    g_up(k, s).wait_recv()

                @pl.when(here & (z <= r) & (z > 0))
                def _(k=k, s=s):
                    g_dn(k, s).start()

                @pl.when(here & (z >= r) & (z < nz - 1))
                def _(k=k, s=s):
                    g_up(k, s).start()

                @pl.when(here)
                def _(k=k, s=s):
                    g_first(k, s).start()

                k = i - (lag + 1)
                here = ok(k) & (k % 2 == e)

                @pl.when(here)
                def _(k=k, s=s):
                    cp = g_first(k, s)
                    cp.wait_send()
                    cp.wait_recv()

                @pl.when(here & (z <= r) & (z > 0))
                def _(k=k, s=s):
                    g_dn(k, s).wait_send()

                @pl.when(here & (z >= r) & (z < nz - 1))
                def _(k=k, s=s):
                    g_up(k, s).wait_send()


KINDS = {"F": (2, W), "U": (2, 2, W), "D": (2, 2, W), "L": (2, W), "M": (2, W), "V": (2, 2, W), "E": (2, 2, W), "G": (2, 2, W)}
SEMS = [k + e for k in KINDS for e in "sr"]


def comm_scratch(width):
    return [
        pltpu.VMEM((2, W, R // 2, width), jnp.float32),
        pltpu.VMEM((2, 2, W, R // 4, width), jnp.float32),
        pltpu.VMEM((2, 2, W, R // 4, width), jnp.float32),
        pltpu.VMEM((2, W, R // 8, width), jnp.float32),
    ] + [pltpu.SemaphoreType.DMA(KINDS[k[0]]) for k in SEMS]

def f32dot(a, b, dims=((1,), (0,))):
    return lax.dot_general(a, b, (dims, ((), ())), preferred_element_type=jnp.float32)


NT = ((1,), (1,))
TN = ((0,), (0,))


def tables(tokens):
    half = HEAD // 2
    frequency = np.exp(np.arange(half) * (-2.0 * math.log(10000.0) / HEAD)).astype(np.float32)
    angles = (np.arange(tokens, dtype=np.float32)[:, None] * frequency[None, :]).astype(np.float64)
    cosine = np.tile(np.cos(angles), (1, LANES // half)).astype(np.float32)
    sign = np.where((np.arange(LANES) // half) % 2 == 0, -1.0, 1.0)
    sine = (np.tile(np.sin(angles), (1, LANES // half)) * sign).astype(np.float32)
    return cosine, sine


def swap_halves(v, low):
    return jnp.where(low, pltpu.roll(v, LANES - HEAD // 2, 1), pltpu.roll(v, HEAD // 2, 1))


def chunks(total, size, body, unroll=False):
    count = total // size

    def one(i, carry):
        body(pl.multiple_of(i * size, size))
        return carry

    lax.fori_loop(0, count, one, 0, unroll=unroll)


def mean_of(v):
    return jnp.mean(v, axis=-1, keepdims=True)


def norm(v):
    centred = v - mean_of(v)
    inv = lax.rsqrt(mean_of(centred * centred) + EPSILON)
    return centred * inv, inv


class Row:
    def __init__(self, ref):
        self.ref = ref

    def __getitem__(self, index):
        v = self.ref[...] if index is Ellipsis else self.ref[index[1]]
        return v.reshape(1, v.shape[0])


def layer_kernel(n, *refs):
    (x_h, ids, ag_h, as_h, wp_h, pb_h, wo_h, ob_h, fg_h, fs_h, we_h, eb_h, ws_h, sb_h, go_h, cos_h, sin_h) = refs[:17]
    O, bo, gi = refs[17:20]
    (x, ag, ash, wp, pb, wo, ob, fg, fs, we, eb, ws, sb, go, cos, sin) = refs[20:36]
    ag, ash, ob, fg, fs, eb, sb = (Row(v) for v in (ag, ash, ob, fg, fs, eb, sb))
    (ain, qkv, att, prob, mid, ein, act, PX, RX, dqkv, G, RF, RU, RD, RL, local, xs, xr) = refs[36:54]
    sems = dict(zip(SEMS, refs[54:]))
    T, D = x.shape
    WL = wo.shape[0]
    FL = ws.shape[0]
    half = T // 2
    parts = WL // LANES
    base_out, base_pack = FL + D * (FL // D), FL + D * (FL // D) + WL
    base_small = base_pack + D + WL
    full = base_small // (2 * R)
    comm = Comm(n, (full + 1, full), G, O, RF, RU, RD, RL, sems)
    at_step = [0]

    def tick(count=1):
        if count == 1:
            comm.step(jnp.int32(at_step[0]))
        else:

            def one(i, carry):
                comm.step(i)
                return carry

            lax.fori_loop(at_step[0], at_step[0] + count, one, 0)
        at_step[0] += count


    loads = []
    for j, (src, dst) in enumerate(
        [(x_h, x), (wp_h, wp), (cos_h, cos), (sin_h, sin), (ag_h, ag.ref), (as_h, ash.ref), (pb_h, pb), (wo_h, wo), (ob_h, ob.ref), (fg_h, fg.ref), (fs_h, fs.ref), (we_h, we), (eb_h, eb.ref), (go_h, go), (ws_h, ws), (sb_h, sb.ref)]
    ):
        cp = pltpu.make_async_copy(src, dst, local.at[j])
        cp.start()
        loads.append(cp)
    comm.barrier()
    for j in (0, 4, 5):
        loads[j].wait()

    lane = lax.broadcasted_iota(jnp.int32, (1, LANES), 1)
    low_half = (lane // (HEAD // 2)) % 2 == 0
    first_head = lane < HEAD
    other = (ids[T - 1] > 0).astype(jnp.float32)
    col = lax.broadcasted_iota(jnp.int32, (1, T), 1)
    top_bias = jnp.where(col < half, 0.0, MASKED * other)
    low_bias = jnp.where(col < half, MASKED * other, 0.0)

    for j in (2, 3):
        loads[j].wait()
    for table in (cos, sin):
        table[pl.ds(half, half), :] = table[pl.ds(half, half), :] * (1.0 - other) + table[pl.ds(0, half), :] * other

    def pre_part(p):
        return G.at[pl.ds(base_pack + p * T, T), :]

    def norm_in(r):
        rows = pl.ds(r, 64)
        normed, _ = norm(x[rows, :].astype(jnp.float32))
        ain[rows, :] = (normed * ag[...] + ash[...]).astype(jnp.bfloat16)

    chunks(T, 64, norm_in)
    for j in (1, 6):
        loads[j].wait()
    tmp = PX.at[0]
    for c in range(3):
        tmp[:, pl.ds(0, WL)] = f32dot(ain[...], wp[c])

        def turn(r, c=c):
            rows = pl.ds(r, 64)
            for j in range(parts):
                v = tmp[rows, pl.ds(j * LANES, LANES)] + pb[pl.ds(c, 1), pl.ds(j * LANES, LANES)]
                if c < 2:
                    v = v * cos[rows, :] + swap_halves(v, low_half) * sin[rows, :]
                if c == 0:
                    v = v.astype(jnp.bfloat16) * jnp.bfloat16(HEAD**-0.5)
                qkv[c * parts + j, rows, :] = v.astype(jnp.bfloat16)

        chunks(T, 64, turn)

    QR = 128

    def attend(j, carry):
        keys, vals = qkv[parts + j], qkv[2 * parts + j]
        for r in range(0, T, QR):
            q = qkv[j, r : r + QR, :]
            bias = top_bias if r < half else low_bias
            outs = []
            for e in (0, 1):
                qm = jnp.where(first_head if e == 0 else ~first_head, q, jnp.zeros_like(q))
                s = f32dot(qm, keys, NT) + bias
                p = jnp.exp(s - jnp.max(s, axis=-1, keepdims=True))
                p = (p * (1.0 / jnp.sum(p, axis=-1, keepdims=True))).astype(jnp.bfloat16)
                prob[2 * j + e, r : r + QR, :] = p
                outs.append(f32dot(p, vals))
            att[r : r + QR, pl.ds(pl.multiple_of(j * LANES, LANES), LANES)] = jnp.where(first_head, *outs).astype(jnp.bfloat16)
        return carry

    lax.fori_loop(0, parts, attend, 0)

    def swap(i, h):
        rows = pl.ds(h * half, half)
        return pltpu.make_async_remote_copy(
            src_ref=PX.at[i % 2, rows, :], dst_ref=RX.at[i % 2, rows, :], send_sem=xs.at[i, h], recv_sem=xr.at[i, h],
            device_id=(comm.d, 1 - comm.t), device_id_type=MESH)

    for j in (7, 8, 9, 10):
        loads[j].wait()
    for h in (0, 1):
        rows = pl.ds(h * half, half)
        PX[0, rows, :] = f32dot(att[rows, :], wo[...])
        swap(0, h).start()
    for h in (0, 1):
        swap(0, h).wait_recv()

        def middle_rows(r, h=h):
            rows = pl.ds(h * half + r, 64)
            v = x[rows, :].astype(jnp.float32) + (PX[0, rows, :] + RX[0, rows, :]) + ob[...]
            mid[rows, :] = v
            normed, _ = norm(v)
            ein[rows, :] = (normed * fg[...] + fs[...]).astype(jnp.bfloat16)

        chunks(half, 64, middle_rows)
    for j in (11, 12):
        loads[j].wait()

    NB = WL
    per = D // NB

    for b in range(FL // NB):
        cols = pl.ds(b * NB, NB)
        here = pl.ds((b % per) * NB, NB)
        pre = pre_part(b // per)
        pre[:, here] = f32dot(ein[...], we[:, cols])

        def gelu_rows(r, pre=pre, here=here, cols=cols):
            rows = pl.ds(r, 64)
            v = pre[rows, here] + eb[:, cols]
            pre[rows, here] = v
            act[rows, cols] = (v * (0.5 + 0.5 * lax.erf(v * math.sqrt(0.5)))).astype(jnp.bfloat16)

        chunks(T, 64, gelu_rows)
    loads[13].wait()
    for b in range(FL // NB):
        G[pl.ds(b * NB, NB), :] = f32dot(act[:, pl.ds(b * NB, NB)], go[...], TN)
    tick(2)
    swap(0, 0).wait_send()
    swap(0, 1).wait_send()
    for j in (14, 15):
        loads[j].wait()

    for h in (0, 1):
        rows = pl.ds(h * half, half)
        PX[1, rows, :] = f32dot(act[rows, :], ws[...])
        swap(1, h).start()
    tick()
    for h in (0, 1):
        swap(1, h).wait()

        def out_rows(r, h=h):
            rows = pl.ds(h * half + r, 64)
            bo[rows, :] = (mid[rows, :] + (PX[1, rows, :] + RX[1, rows, :]) + sb[...]).astype(jnp.bfloat16)

        chunks(half, 64, out_rows)
        tick()

    def small_row(k):
        return G.at[pl.ds(base_small + k, 1), :]

    for b in range(FL // NB):
        cols = pl.ds(b * NB, NB)
        here = pl.ds((b % per) * NB, NB)
        pre = pre_part(b // per)
        PX[0, :, pl.ds(0, NB)] = f32dot(go[...], ws[cols, :], NT)

        def slope_rows(i, total, pre=pre, here=here, cols=cols):
            rows = pl.ds(pl.multiple_of(i * 64, 64), 64)
            v = pre[rows, here]
            slope = 0.5 + 0.5 * lax.erf(v * math.sqrt(0.5)) + v * (jnp.exp(v * v * -0.5) * (1.0 / math.sqrt(2.0 * math.pi)))
            g = (PX[0, rows, pl.ds(0, NB)] * slope).astype(jnp.bfloat16)
            act[rows, cols] = g
            return total + jnp.sum(g.astype(jnp.float32), axis=0, keepdims=True)

        total = lax.fori_loop(0, T // 64, slope_rows, jnp.zeros((1, NB), jnp.float32))
        G[pl.ds(base_small + 6 + b // per, 1), here] = total
        tick()
    for p in range(FL // D):
        for b in range(D // NB):
            G[pl.ds(FL + p * D + b * NB, NB), :] = f32dot(ein[:, pl.ds(b * NB, NB)], act[:, pl.ds(p * D, D)], TN)
        tick()

    for h in (0, 1):
        rows = pl.ds(h * half, half)
        PX[0, rows, :] = f32dot(act[rows, :], we[...], NT)
        swap(2, h).start()
    tick()

    zero = jnp.zeros((1, D), jnp.float32)
    sums = (zero, zero, zero, zero)
    for h in (0, 1):
        swap(2, h).wait()

        def back_rows(i, totals, h=h):
            rows = pl.ds(pl.multiple_of(h * half + i * 32, 32), 32)
            gain_sum, shift_sum, bias_sum, top_sum = totals
            g = PX[0, rows, :] + RX[0, rows, :]
            normed, inv = norm(mid[rows, :])
            scaled = g * fg[...]
            top = go[rows, :].astype(jnp.float32)
            gm = top + (scaled - mean_of(scaled) - normed * mean_of(scaled * normed)) * inv
            mid[rows, :] = gm
            ein[rows, :] = gm.astype(jnp.bfloat16)
            return (
                gain_sum + jnp.sum(g * normed, axis=0, keepdims=True),
                shift_sum + jnp.sum(g, axis=0, keepdims=True),
                bias_sum + jnp.sum(gm, axis=0, keepdims=True),
                top_sum + jnp.sum(top, axis=0, keepdims=True),
            )

        sums = lax.fori_loop(0, half // 32, back_rows, sums)
        tick()
    for k, v in zip((3, 4, 2, 5), sums):
        small_row(k)[...] = v

    G[pl.ds(base_out, WL), :] = f32dot(att[...], ein[...], TN)
    tick()
    att[...] = f32dot(ein[...], wo[...], NT).astype(jnp.bfloat16)

    def attend_back(j, carry):
        keys, vals, queries = qkv[parts + j], qkv[2 * parts + j], qkv[j]
        at = pl.ds(pl.multiple_of(j * LANES, LANES), LANES)
        dv = [None, None]
        dk = [None, None]
        for r in range(0, T, QR):
            rows = pl.ds(r, QR)
            do = att[rows, at]
            q = qkv[j, rows, :]
            dq = []
            for e in (0, 1):
                dom = jnp.where(first_head if e == 0 else ~first_head, do, jnp.zeros_like(do))
                p_low = prob[2 * j + e, rows, :]
                p = p_low.astype(jnp.float32)
                dp = f32dot(dom, vals, NT)
                inner = jnp.sum(p * dp, axis=-1, keepdims=True)
                ds = (p * (dp - inner)).astype(jnp.bfloat16)
                dq.append(f32dot(ds, keys))
                add_v = f32dot(p_low, do, TN)
                add_k = f32dot(ds, q, TN)
                dv[e] = add_v if r == 0 else dv[e] + add_v
                dk[e] = add_k if r == 0 else dk[e] + add_k
            v = jnp.where(first_head, *dq) * (HEAD**-0.5)
            dqkv[j, rows, :] = (v * cos[rows, :] - swap_halves(v, low_half) * sin[rows, :]).astype(jnp.bfloat16)
            if (r // QR) % 2 == 1:
                comm.step(at_step[0] + 2 * j + r // (2 * QR))
        dqkv[2 * parts + j] = jnp.where(first_head, *dv).astype(jnp.bfloat16)
        v = jnp.where(first_head, *dk)
        dqkv[parts + j] = (v * cos[...] - swap_halves(v, low_half) * sin[...]).astype(jnp.bfloat16)
        return carry

    lax.fori_loop(0, parts, attend_back, 0)
    at_step[0] += 2 * parts

    for c in range(3):
        for j in range(parts):
            g = dqkv[c * parts + j]
            cols = pl.ds(j * LANES, LANES)
            G[pl.ds(base_small + 8 + c, 1), cols] = jnp.sum(g.astype(jnp.float32), axis=0, keepdims=True)
            grad = f32dot(ain[...], g, TN)
            if c < 2:
                G[pl.ds(base_pack, D), pl.ds(c * WL + j * LANES, LANES)] = grad
            else:
                for p in range(2):
                    G[pl.ds(base_pack + D, WL), pl.ds(p * WL + j * LANES, LANES)] = grad[p * WL : (p + 1) * WL, :]
        tick()

    for h in (0, 1):
        rows = pl.ds(h * half, half)
        acc = None
        for c in range(3):
            for j in range(parts):
                term = f32dot(dqkv[c * parts + j, rows, :], wp[c, :, pl.ds(j * LANES, LANES)], NT)
                acc = term if acc is None else acc + term
        PX[1, rows, :] = acc
        swap(3, h).start()
    tick()
    sums = (zero, zero)
    for h in (0, 1):
        swap(3, h).wait()

        def input_rows(i, totals, h=h):
            rows = pl.ds(pl.multiple_of(h * half + i * 32, 32), 32)
            g = PX[1, rows, :] + RX[1, rows, :]
            normed, inv = norm(x[rows, :].astype(jnp.float32))
            scaled = g * ag[...]
            v = mid[rows, :] + (scaled - mean_of(scaled) - normed * mean_of(scaled * normed)) * inv
            gi[rows, :] = v.astype(jnp.bfloat16)
            return (
                totals[0] + jnp.sum(g * normed, axis=0, keepdims=True),
                totals[1] + jnp.sum(g, axis=0, keepdims=True),
            )

        sums = lax.fori_loop(0, half // 32, input_rows, sums)
        tick()
    small_row(0)[...] = sums[0]
    small_row(1)[...] = sums[1]
    G[pl.ds(base_small + 8, 3), pl.ds(WL, D - WL)] = jnp.zeros((3, D - WL), jnp.float32)
    G[pl.ds(base_small + 11, R - 11), :] = jnp.zeros((R - 11, D), jnp.float32)

    tick(comm.steps() - at_step[0])


def unpack(moves_of, whole_ref, bo_ref, gi_ref, *refs):
    outs, local = refs[:-1], refs[-1]
    stores = []
    pairs, rows = moves_of(whole_ref, bo_ref, gi_ref, outs)
    for pair in pairs:
        cp = pltpu.make_async_copy(*pair, local.at[len(stores)])
        cp.start()
        stores.append(cp)
    for src, dst in rows:
        dst[...] = src[...]
    for cp in stores:
        cp.wait()


def unpack_moves(T, D, WL, FL, O, bo, gi, outs):
    base_out = FL + D * (FL // D)
    base_pack = base_out + WL
    base_small = base_pack + D + WL
    pairs = [(bo, outs[0]), (gi, outs[1]), (O.at[pl.ds(0, FL), :], outs[2])]
    for p in range(FL // D):
        pairs.append((O.at[pl.ds(FL + p * D, D), :], outs[3].at[:, pl.ds(p * D, D)]))
    pairs.append((O.at[pl.ds(base_out, WL), :], outs[4]))
    for c in range(2):
        pairs.append((O.at[pl.ds(base_pack, D), pl.ds(c * WL, WL)], outs[5].at[c]))
    for p in range(2):
        pairs.append((O.at[pl.ds(base_pack + D, WL), pl.ds(p * WL, WL)], outs[5].at[2, pl.ds(p * WL, WL), :]))
    rows = [(O.at[base_small + k, :], outs[6 + k]) for k in range(6)]
    for p in range(FL // D):
        rows.append((O.at[base_small + 6 + p, :], outs[12].at[pl.ds(p * D, D)]))
    rows.append((O.at[pl.ds(base_small + 8, 3), pl.ds(0, WL)], outs[13]))
    return pairs, rows


def body(
    n_dp,
    block_input,
    sequence_ids,
    attention_gain,
    attention_shift,
    packed_weight,
    packed_bias,
    output_weight,
    output_bias,
    feedforward_gain,
    feedforward_shift,
    expand_weight,
    expand_bias,
    shrink_weight,
    shrink_bias,
    grad_output,
):
    T, D = block_input.shape
    WL = packed_weight.shape[2]
    FL = shrink_weight.shape[0]
    parts = WL // LANES
    bf16, f32 = jnp.bfloat16, jnp.float32
    cosine, sine = tables(T)
    total = FL + D * (FL // D) + WL + D + WL + R

    args = [
        block_input,
        sequence_ids,
        attention_gain,
        attention_shift,
        jnp.transpose(packed_weight, (1, 0, 2)),
        packed_bias,
        output_weight,
        output_bias,
        feedforward_gain,
        feedforward_shift,
        expand_weight,
        expand_bias,
        shrink_weight,
        shrink_bias,
        grad_output,
        jnp.asarray(cosine),
        jnp.asarray(sine),
    ]
    hbm = pl.BlockSpec(memory_space=pltpu.HBM)
    vmem = pl.BlockSpec(memory_space=pltpu.VMEM)
    held = [pltpu.VMEM(a.shape, a.dtype) for i, a in enumerate(args) if i != 1]
    scratch = comm_scratch(D)
    whole, out, grad_in = pl.pallas_call(
        functools.partial(layer_kernel, n_dp),
        out_shape=[pltpu.VMEM((total, D), f32), pltpu.VMEM((T, D), bf16), pltpu.VMEM((T, D), bf16)],
        in_specs=[hbm, pl.BlockSpec(memory_space=pltpu.SMEM)] + [hbm] * 15,
        out_specs=[vmem] * 3,
        scratch_shapes=held
        + [
            pltpu.VMEM((T, D), bf16),
            pltpu.VMEM((3 * parts, T, LANES), bf16),
            pltpu.VMEM((T, WL), bf16),
            pltpu.VMEM((2 * parts, T, T), bf16),
            pltpu.VMEM((T, D), f32),
            pltpu.VMEM((T, D), bf16),
            pltpu.VMEM((T, FL), bf16),
            pltpu.VMEM((2, T, D), f32),
            pltpu.VMEM((2, T, D), f32),
            pltpu.VMEM((3 * parts, T, LANES), bf16),
            pltpu.VMEM((total, D), f32),
        ]
        + scratch[:4]
        + [pltpu.SemaphoreType.DMA((16,)), pltpu.SemaphoreType.DMA((4, 2)), pltpu.SemaphoreType.DMA((4, 2))]
        + scratch[4:],
        compiler_params=pltpu.CompilerParams(
            collective_id=0, has_side_effects=True, vmem_limit_bytes=48 << 20
        ),
    )(*args)
    shapes = [
        ((T, D), bf16),
        ((T, D), bf16),
        ((FL, D), f32),
        ((D, FL), f32),
        ((WL, D), f32),
        ((3, D, WL), f32),
        *[((D,), f32)] * 6,
        ((FL,), f32),
        ((3, WL), f32),
    ]
    anywhere = pl.BlockSpec(memory_space=pl.ANY)
    got = pl.pallas_call(
        functools.partial(unpack, functools.partial(unpack_moves, T, D, WL, FL)),
        out_shape=[pltpu.HBM(*s) for s in shapes[:6]] + [jax.ShapeDtypeStruct(*s) for s in shapes[6:]],
        in_specs=[vmem] * 3,
        out_specs=[anywhere] * 6 + [vmem] * 8,
        scratch_shapes=[pltpu.SemaphoreType.DMA((32,))],
        compiler_params=pltpu.CompilerParams(vmem_limit_bytes=1 << 20),
    )(whole, out, grad_in)
    small = got[6:12]
    return (
        got[0],
        got[1],
        small[0],
        small[1],
        jnp.transpose(got[5], (1, 0, 2)),
        got[13],
        got[4],
        small[2],
        small[3],
        small[4],
        got[3],
        got[12],
        got[2],
        small[5],
    )


def solution(mesh):
    in_specs = (
        P("dp", None),
        P("dp"),
        P(),
        P(),
        P(None, None, "tensor"),
        P(None, "tensor"),
        P("tensor", None),
        P(),
        P(),
        P(),
        P(None, "tensor"),
        P("tensor"),
        P("tensor", None),
        P(),
        P("dp", None),
    )
    out_specs = (
        P("dp", None),
        P("dp", None),
        P(),
        P(),
        P(None, None, "tensor"),
        P(None, "tensor"),
        P("tensor", None),
        P(),
        P(),
        P(),
        P(None, "tensor"),
        P("tensor"),
        P("tensor", None),
        P(),
    )
    return jax.shard_map(
        functools.partial(body, mesh.shape["dp"]), mesh=mesh, in_specs=in_specs, out_specs=out_specs, check_vma=False
    )
```

```python
import functools
import math

import jax
import jax.numpy as jnp
import numpy as np
from jax import lax
from jax.experimental import pallas as pl
from jax.experimental.pallas import tpu as pltpu
from jax.sharding import PartitionSpec as P

HEAD = 64
EPSILON = 1e-05
MASKED = -1000000000.0
LANES = 128
MESH = pl.DeviceIdType.MESH
W = 8
R = 64
LF = 2


class Comm:
    def __init__(self, n, counts, G, O, RF, RU, RD, RL, sems):
        self.nz = n // 4
        self.counts = counts
        self.G, self.O, self.RF, self.RU, self.RD, self.RL = G, O, RF, RU, RD, RL
        self.sems = sems
        d = lax.axis_index("dp")
        self.t = lax.axis_index("tensor")
        self.d = d
        self.z = d // 4
        self.y = (d // 2) % 2
        self.x = d % 2
        self.px = d + 1 - 2 * self.x
        self.py = d + 2 - 4 * self.y

    def steps(self):
        return max(self.counts) + LF + 2 * self.nz + 3

    def arrive(self):
        b = pltpu.get_barrier_semaphore()
        for peer in ((self.px, self.t), (self.py, self.t), (self.d, 1 - self.t)):
            pl.semaphore_signal(b, inc=1, device_id=peer, device_id_type=MESH)

        @pl.when(self.z > 0)
        def _():
            pl.semaphore_signal(b, inc=1, device_id=(self.d - 4, self.t), device_id_type=MESH)

        @pl.when(self.z < self.nz - 1)
        def _():
            pl.semaphore_signal(b, inc=1, device_id=(self.d + 4, self.t), device_id_type=MESH)

    def ready(self):
        edge = (self.z > 0).astype(jnp.int32) + (self.z < self.nz - 1).astype(jnp.int32)
        pl.semaphore_wait(pltpu.get_barrier_semaphore(), 3 + edge)

    def rows(self, start, size):
        return self.G.at[pl.ds(pl.multiple_of(start, 8), size), :]

    def done(self, start, size):
        return self.O.at[pl.ds(pl.multiple_of(start, 8), size), :]

    def copy(self, src, dst, kind, idx, dev):
        return pltpu.make_async_remote_copy(
            src_ref=src, dst_ref=dst, send_sem=self.sems[kind + "s"].at[idx], recv_sem=self.sems[kind + "r"].at[idx],
            device_id=(dev, self.t), device_id_type=MESH)

    def add(self, start, size, buf):
        r = self.rows(start, size)
        r[...] = r[...] + buf[...]

    def step(self, i):
        for c in (0, 1):
            self.first(c, i)
        for c in (0, 1):
            self.rest(c, i)

    def base(self, c, k):
        return (2 * k + c) * R

    def f_copy(self, c, k):
        a, dev = (self.x, self.px) if c == 0 else (self.y, self.py)
        q = k % W
        return self.copy(self.rows(self.base(c, k) + (1 - a) * (R // 2), R // 2), self.RF.at[c, q], "F", (c, q), dev)

    def first(self, c, i):
        @pl.when(i < self.counts[c])
        def _():
            self.f_copy(c, i).start()

    def rest(self, c, i):
        nz, z = self.nz, self.z
        a, fdev, b, ldev = (self.x, self.px, self.y, self.py) if c == 0 else (self.y, self.py, self.x, self.px)
        n = self.counts[c]
        H, Q, E = R // 2, R // 4, R // 8

        def ok(k):
            return (k >= 0) & (k < n)

        def half(k):
            return self.base(c, k) + a * H

        def sub(k, s):
            return half(k) + s * Q

        def root(k, s):
            return k % 2 if s == 0 else nz - 1 - k % 2

        k = i - LF

        @pl.when(ok(k))
        def _(k=k):
            cp = self.f_copy(c, k)
            cp.wait_send()
            cp.wait_recv()
            self.add(half(k), H, self.RF.at[c, k % W])

        def up(k, s):
            return self.copy(self.rows(sub(k, s), Q), self.RU.at[c, s, k % W], "U", (c, s, k % W), jnp.minimum(self.d + 4, 4 * nz - 1))

        def dn(k, s):
            return self.copy(self.rows(sub(k, s), Q), self.RD.at[c, s, k % W], "D", (c, s, k % W), jnp.maximum(self.d - 4, 0))

        for s in (0, 1):
            k = i - (LF + z)

            @pl.when(ok(k) & (z <= root(k, s)) & (z > 0))
            def _(k=k, s=s):
                up(k, s).wait_recv()
                self.add(sub(k, s), Q, self.RU.at[c, s, k % W])

            @pl.when(ok(k) & (z < root(k, s)))
            def _(k=k, s=s):
                up(k, s).start()

            k = i - (LF + nz - 1 - z)

            @pl.when(ok(k) & (z >= root(k, s)) & (z < nz - 1))
            def _(k=k, s=s):
                dn(k, s).wait_recv()
                self.add(sub(k, s), Q, self.RD.at[c, s, k % W])

            @pl.when(ok(k) & (z > root(k, s)))
            def _(k=k, s=s):
                dn(k, s).start()

            k = i - (LF + z + 1)

            @pl.when(ok(k) & (z < root(k, s)))
            def _(k=k, s=s):
                up(k, s).wait_send()

            k = i - (LF + nz - 1 - z + 1)

            @pl.when(ok(k) & (z > root(k, s)))
            def _(k=k, s=s):
                dn(k, s).wait_send()

        def last(k, s):
            return self.copy(self.rows(sub(k, s) + (1 - b) * E, E), self.RL.at[c, k % W], "L", (c, k % W), ldev)

        def last_back(k, s):
            at = sub(k, s) + b * E
            return self.copy(self.rows(at, E), self.done(at, E), "M", (c, k % W), ldev)

        for s in (0, 1):
            k = i - (LF + nz - 1)

            @pl.when(ok(k) & (z == root(k, s)))
            def _(k=k, s=s):
                last(k, s).start()

            k = i - (LF + nz)

            @pl.when(ok(k) & (z == root(k, s)))
            def _(k=k, s=s):
                cp = last(k, s)
                cp.wait_send()
                cp.wait_recv()
                self.add(sub(k, s) + b * E, E, self.RL.at[c, k % W])
                last_back(k, s).start()
                self.done(sub(k, s) + b * E, E)[...] = self.rows(sub(k, s) + b * E, E)[...]

        def g_up(k, s):
            r = self.done(sub(k, s), Q)
            return self.copy(r, r, "V", (c, s, k % W), jnp.minimum(self.d + 4, 4 * nz - 1))

        def g_dn(k, s):
            r = self.done(sub(k, s), Q)
            return self.copy(r, r, "E", (c, s, k % W), jnp.maximum(self.d - 4, 0))

        def g_first(k, s):
            r = self.done(sub(k, s), Q)
            return self.copy(r, r, "G", (c, s, k % W), fdev)

        for e in (0, 1):
            for s in (0, 1):
                r = e if s == 0 else nz - 1 - e
                lag = LF + nz + 1 + jnp.abs(z - r)
                k = i - lag
                here = ok(k) & (k % 2 == e)

                @pl.when(here & (z == r))
                def _(k=k, s=s):
                    cp = last_back(k, s)
                    cp.wait_send()
                    cp.wait_recv()

                @pl.when(here & (z < r))
                def _(k=k, s=s):
                    g_dn(k, s).wait_recv()

                @pl.when(here & (z > r))
                def _(k=k, s=s):
                    g_up(k, s).wait_recv()

                @pl.when(here & (z <= r) & (z > 0))
                def _(k=k, s=s):
                    g_dn(k, s).start()

                @pl.when(here & (z >= r) & (z < nz - 1))
                def _(k=k, s=s):
                    g_up(k, s).start()

                @pl.when(here)
                def _(k=k, s=s):
                    g_first(k, s).start()

                k = i - (lag + 1)
                here = ok(k) & (k % 2 == e)

                @pl.when(here)
                def _(k=k, s=s):
                    cp = g_first(k, s)
                    cp.wait_send()
                    cp.wait_recv()

                @pl.when(here & (z <= r) & (z > 0))
                def _(k=k, s=s):
                    g_dn(k, s).wait_send()

                @pl.when(here & (z >= r) & (z < nz - 1))
                def _(k=k, s=s):
                    g_up(k, s).wait_send()


KINDS = {"F": (2, W), "U": (2, 2, W), "D": (2, 2, W), "L": (2, W), "M": (2, W), "V": (2, 2, W), "E": (2, 2, W), "G": (2, 2, W)}
SEMS = [k + e for k in KINDS for e in "sr"]


def comm_scratch(width):
    return [
        pltpu.VMEM((2, W, R // 2, width), jnp.float32),
        pltpu.VMEM((2, 2, W, R // 4, width), jnp.float32),
        pltpu.VMEM((2, 2, W, R // 4, width), jnp.float32),
        pltpu.VMEM((2, W, R // 8, width), jnp.float32),
    ] + [pltpu.SemaphoreType.DMA(KINDS[k[0]]) for k in SEMS]

def f32dot(a, b, dims=((1,), (0,))):
    return lax.dot_general(a, b, (dims, ((), ())), preferred_element_type=jnp.float32)


NT = ((1,), (1,))
TN = ((0,), (0,))


def tables(tokens):
    half = HEAD // 2
    frequency = np.exp(np.arange(half) * (-2.0 * math.log(10000.0) / HEAD)).astype(np.float32)
    angles = (np.arange(tokens, dtype=np.float32)[:, None] * frequency[None, :]).astype(np.float64)
    cosine = np.tile(np.cos(angles), (1, LANES // half)).astype(np.float32)
    sign = np.where((np.arange(LANES) // half) % 2 == 0, -1.0, 1.0)
    sine = (np.tile(np.sin(angles), (1, LANES // half)) * sign).astype(np.float32)
    return cosine, sine


def swap_halves(v, low):
    return jnp.where(low, pltpu.roll(v, LANES - HEAD // 2, 1), pltpu.roll(v, HEAD // 2, 1))


def chunks(total, size, body, unroll=False):
    count = total // size

    def one(i, carry):
        body(pl.multiple_of(i * size, size))
        return carry

    lax.fori_loop(0, count, one, 0, unroll=unroll)


def mean_of(v):
    return jnp.mean(v, axis=-1, keepdims=True)


def norm(v):
    centred = v - mean_of(v)
    inv = lax.rsqrt(mean_of(centred * centred) + EPSILON)
    return centred * inv, inv


class Row:
    def __init__(self, ref):
        self.ref = ref

    def __getitem__(self, index):
        v = self.ref[...] if index is Ellipsis else self.ref[index[1]]
        return v.reshape(1, v.shape[0])


def layer_kernel(n, *refs):
    (x_h, ids, ag_h, as_h, wp_h, pb_h, wo_h, ob_h, fg_h, fs_h, we_h, eb_h, ws_h, sb_h, go_h, cos_h, sin_h) = refs[:17]
    O, bo, gi = refs[17:20]
    (x, ag, ash, wp, pb, wo, ob, fg, fs, we, eb, ws, sb, go, cos, sin) = refs[20:36]
    ag, ash, ob, fg, fs, eb, sb = (Row(v) for v in (ag, ash, ob, fg, fs, eb, sb))
    (ain, qkv, att, prob, mid, ein, act, PX, RX, dqkv, G, RF, RU, RD, RL, local, xs, xr, ys, yr, bias2) = refs[36:57]
    sems = dict(zip(SEMS, refs[57:]))
    T, D = x.shape
    WL = wo.shape[0]
    FL = ws.shape[0]
    half = T // 2
    parts = WL // LANES
    base_out, base_pack = FL + D * (FL // D), FL + D * (FL // D) + WL
    base_small = base_pack + D + WL
    full = base_small // (2 * R)
    comm = Comm(n, (full + 1, full), G, O, RF, RU, RD, RL, sems)
    at_step = [0]

    def tick(more=0):
        comm.step(jnp.int32(at_step[0]) + more)

    def passed(count):
        at_step[0] += count

    loads = []
    for j, (src, dst) in enumerate(
        [(x_h, x), (wp_h.at[0], wp.at[0]), (cos_h, cos), (sin_h, sin), (ag_h, ag.ref), (as_h, ash.ref), (pb_h, pb), (wo_h, wo), (ob_h, ob.ref), (fg_h, fg.ref), (fs_h, fs.ref), (we_h, we), (eb_h, eb.ref), (go_h, go), (ws_h, ws), (sb_h, sb.ref), (wp_h.at[1], wp.at[1]), (wp_h.at[2], wp.at[2])]
    ):
        loads.append(pltpu.make_async_copy(src, dst, local.at[j]))

    def begin(*which):
        for j in which:
            loads[j].start()

    def arrived(*which):
        for j in which:
            loads[j].wait()

    begin(0, 4, 5, 1, 2, 3, 6, 16, 17)
    comm.arrive()
    arrived(0, 4, 5)

    lane = lax.broadcasted_iota(jnp.int32, (1, LANES), 1)
    low_half = (lane // (HEAD // 2)) % 2 == 0
    first_head = lane < HEAD
    other = (ids[T - 1] > 0).astype(jnp.float32)
    col = lax.broadcasted_iota(jnp.int32, (1, T), 1)
    top_bias = jnp.where(col < half, 0.0, MASKED * other)
    low_bias = jnp.where(col < half, MASKED * other, 0.0)

    def pre_part(p):
        return G.at[pl.ds(pl.multiple_of(base_pack + p * T, 8), T), :]

    def norm_in(r):
        rows = pl.ds(r, 64)
        normed, _ = norm(x[rows, :].astype(jnp.float32))
        ain[rows, :] = (normed * ag[...] + ash[...]).astype(jnp.bfloat16)

    chunks(T, 64, norm_in)
    arrived(1, 2, 3, 6)
    begin(7, 8, 9, 10, 11, 12, 13, 14, 15)
    for table in (cos, sin):
        table[pl.ds(half, half), :] = table[pl.ds(half, half), :] * (1.0 - other) + table[pl.ds(0, half), :] * other
    tmp = PX.at[0]
    for c in range(3):
        if c > 0:
            arrived(15 + c)
        tmp[:, pl.ds(0, WL)] = f32dot(ain[...], wp[c])

        def turn(r, c=c):
            rows = pl.ds(r, 64)
            for j in range(parts):
                v = tmp[rows, pl.ds(j * LANES, LANES)] + pb[pl.ds(c, 1), pl.ds(j * LANES, LANES)]
                if c < 2:
                    v = v * cos[rows, :] + swap_halves(v, low_half) * sin[rows, :]
                if c == 0:
                    v = v.astype(jnp.bfloat16) * jnp.bfloat16(HEAD**-0.5)
                qkv[c * parts + j, rows, :] = v.astype(jnp.bfloat16)

        chunks(T, 64, turn)

    QR = 128
    blocks = T // QR

    def first_swap(i):
        rows = pl.ds(pl.multiple_of(i * QR, QR), QR)
        return pltpu.make_async_remote_copy(
            src_ref=PX.at[0, rows, :], dst_ref=RX.at[0, rows, :], send_sem=ys.at[i], recv_sem=yr.at[i],
            device_id=(comm.d, 1 - comm.t), device_id_type=MESH)

    def swap(i, h):
        rows = pl.ds(pl.multiple_of(h * half, half), half)
        return pltpu.make_async_remote_copy(
            src_ref=PX.at[i % 2, rows, :], dst_ref=RX.at[i % 2, rows, :], send_sem=xs.at[i, h], recv_sem=xr.at[i, h],
            device_id=(comm.d, 1 - comm.t), device_id_type=MESH)

    arrived(7, 8, 9, 10)
    comm.ready()

    def attend(i, carry):
        rows = pl.ds(pl.multiple_of(i * QR, QR), QR)
        bias = jnp.where(i < blocks // 2, top_bias, low_bias)
        for j in range(parts):
            keys, vals = qkv[parts + j], qkv[2 * parts + j]
            q = qkv[j, rows, :]
            zeros = jnp.zeros_like(q)
            two = jnp.concatenate([jnp.where(first_head, q, zeros), jnp.where(first_head, zeros, q)], axis=0)
            s = f32dot(two, keys, NT) + bias
            p = jnp.exp(s - jnp.max(s, axis=-1, keepdims=True))
            p = (p * (1.0 / jnp.sum(p, axis=-1, keepdims=True))).astype(jnp.bfloat16)
            prob[2 * j, rows, :] = p[:QR]
            prob[2 * j + 1, rows, :] = p[QR:]
            out = f32dot(p, vals)
            att[rows, j * LANES : (j + 1) * LANES] = jnp.where(first_head, out[:QR], out[QR:]).astype(jnp.bfloat16)
        PX[0, rows, :] = f32dot(att[rows, :], wo[...])
        first_swap(i).start()
        return carry

    lax.fori_loop(0, blocks, attend, 0)

    def middle_block(i, carry):
        first_swap(i).wait_recv()

        def middle_rows(r):
            rows = pl.ds(pl.multiple_of(i * QR + r, 64), 64)
            v = x[rows, :].astype(jnp.float32) + (PX[0, rows, :] + RX[0, rows, :]) + ob[...]
            mid[rows, :] = v
            normed, _ = norm(v)
            ein[rows, :] = (normed * fg[...] + fs[...]).astype(jnp.bfloat16)

        chunks(QR, 64, middle_rows, True)
        return carry

    lax.fori_loop(0, blocks, middle_block, 0)
    arrived(11, 12, 13)

    NB = WL
    per = D // NB

    nb = FL // NB
    for b in range(nb):
        bias2[pl.ds(b, 1), :] = eb[:, pl.ds(b * NB, NB)]

    def places(b):
        cols = pl.ds(pl.multiple_of(b * NB, LANES), NB)
        here = pl.ds(pl.multiple_of((b % per) * NB, LANES), NB)
        return cols, here, pre_part(b // per)

    def expand(b, carry):
        cols, here, pre = places(b)
        pre[:, here] = f32dot(ein[...], we[:, cols])

        def gelu_rows(r):
            rows = pl.ds(r, 64)
            v = pre[rows, here] + bias2[pl.ds(b, 1), :]
            pre[rows, here] = v
            act[rows, cols] = (v * (0.5 + 0.5 * lax.erf(v * math.sqrt(0.5)))).astype(jnp.bfloat16)

        chunks(T, 64, gelu_rows)
        G[pl.ds(pl.multiple_of(b * NB, LANES), NB), :] = f32dot(act[:, cols], go[...], TN)
        tick(b)
        return carry

    lax.fori_loop(0, nb, expand, 0)
    passed(nb)
    for i in range(blocks):
        first_swap(i).wait_send()
    arrived(14, 15)

    for h in (0, 1):
        rows = pl.ds(h * half, half)
        PX[1, rows, :] = f32dot(act[rows, :], ws[...])
        swap(1, h).start()

    def out_half(h, carry):
        tick(h)
        swap(1, h).wait()

        def out_rows(r):
            rows = pl.ds(pl.multiple_of(h * half + r, 64), 64)
            bo[rows, :] = (mid[rows, :] + (PX[1, rows, :] + RX[1, rows, :]) + sb[...]).astype(jnp.bfloat16)

        chunks(half, 64, out_rows)
        return carry

    lax.fori_loop(0, 2, out_half, 0)
    passed(2)

    def small_row(k):
        return G.at[pl.ds(base_small + k, 1), :]

    def slope(b, carry):
        cols, here, pre = places(b)
        PX[0, :, pl.ds(0, NB)] = f32dot(go[...], ws[cols, :], NT)

        def slope_rows(i, total):
            rows = pl.ds(pl.multiple_of(i * 64, 64), 64)
            v = pre[rows, here]
            slope = 0.5 + 0.5 * lax.erf(v * math.sqrt(0.5)) + v * (jnp.exp(v * v * -0.5) * (1.0 / math.sqrt(2.0 * math.pi)))
            g = (PX[0, rows, pl.ds(0, NB)] * slope).astype(jnp.bfloat16)
            act[rows, cols] = g
            return total + jnp.sum(g.astype(jnp.float32), axis=0, keepdims=True)

        bias2[pl.ds(b, 1), :] = lax.fori_loop(0, T // 64, slope_rows, jnp.zeros((1, NB), jnp.float32))
        tick(b)
        return carry

    lax.fori_loop(0, nb, slope, 0)
    passed(nb)
    for b in range(nb):
        G[pl.ds(base_small + 6 + b // per, 1), pl.ds((b % per) * NB, NB)] = bias2[pl.ds(b, 1), :]

    def expand_grad(b, carry):
        source = pl.ds(pl.multiple_of((b % per) * NB, LANES), NB)
        wide = pl.ds(pl.multiple_of((b // per) * D, LANES), D)
        G[pl.ds(pl.multiple_of(FL + b * NB, LANES), NB), :] = f32dot(ein[:, source], act[:, wide], TN)
        tick(b)
        return carry

    lax.fori_loop(0, nb, expand_grad, 0)
    passed(nb)

    for h in (0, 1):
        rows = pl.ds(h * half, half)
        PX[0, rows, :] = f32dot(act[rows, :], we[...], NT)
        swap(2, h).start()
    tick()
    passed(1)

    zero = jnp.zeros((1, D), jnp.float32)

    def back_half(h, totals):
        swap(2, h).wait()

        def back_rows(i, totals):
            rows = pl.ds(pl.multiple_of(h * half + i * 32, 32), 32)
            gain_sum, shift_sum, bias_sum, top_sum = totals
            g = PX[0, rows, :] + RX[0, rows, :]
            normed, inv = norm(mid[rows, :])
            scaled = g * fg[...]
            top = go[rows, :].astype(jnp.float32)
            gm = top + (scaled - mean_of(scaled) - normed * mean_of(scaled * normed)) * inv
            mid[rows, :] = gm
            ein[rows, :] = gm.astype(jnp.bfloat16)
            return (
                gain_sum + jnp.sum(g * normed, axis=0, keepdims=True),
                shift_sum + jnp.sum(g, axis=0, keepdims=True),
                bias_sum + jnp.sum(gm, axis=0, keepdims=True),
                top_sum + jnp.sum(top, axis=0, keepdims=True),
            )

        totals = lax.fori_loop(0, half // 32, back_rows, totals)
        tick(h)
        return totals

    sums = lax.fori_loop(0, 2, back_half, (zero, zero, zero, zero))
    passed(2)
    for k, v in zip((3, 4, 2, 5), sums):
        small_row(k)[...] = v

    G[pl.ds(base_out, WL), :] = f32dot(att[...], ein[...], TN)
    att[...] = f32dot(ein[...], wo[...], NT).astype(jnp.bfloat16)
    tick()
    passed(1)

    def attend_back(j, carry):
        keys, vals, queries = qkv[parts + j], qkv[2 * parts + j], qkv[j]
        at = pl.ds(pl.multiple_of(j * LANES, LANES), LANES)
        dv = [None, None]
        dk = [None, None]
        for r in range(0, T, QR):
            rows = pl.ds(r, QR)
            do = att[rows, at]
            q = qkv[j, rows, :]
            dq = []
            for e in (0, 1):
                dom = jnp.where(first_head if e == 0 else ~first_head, do, jnp.zeros_like(do))
                p_low = prob[2 * j + e, rows, :]
                p = p_low.astype(jnp.float32)
                dp = f32dot(dom, vals, NT)
                inner = jnp.sum(p * dp, axis=-1, keepdims=True)
                ds = (p * (dp - inner)).astype(jnp.bfloat16)
                dq.append(f32dot(ds, keys))
                add_v = f32dot(p_low, do, TN)
                add_k = f32dot(ds, q, TN)
                dv[e] = add_v if r == 0 else dv[e] + add_v
                dk[e] = add_k if r == 0 else dk[e] + add_k
            v = jnp.where(first_head, *dq) * (HEAD**-0.5)
            dqkv[j, rows, :] = (v * cos[rows, :] - swap_halves(v, low_half) * sin[rows, :]).astype(jnp.bfloat16)
            if (r // QR) % 2 == 1:
                tick(2 * j + r // (2 * QR))
        dqkv[2 * parts + j] = jnp.where(first_head, *dv).astype(jnp.bfloat16)
        v = jnp.where(first_head, *dk)
        dqkv[parts + j] = (v * cos[...] - swap_halves(v, low_half) * sin[...]).astype(jnp.bfloat16)
        return carry

    lax.fori_loop(0, parts, attend_back, 0)
    passed(2 * parts)

    def joined(c, rows):
        return jnp.concatenate([dqkv[c * parts + j, rows, :] for j in range(parts)], axis=1)

    for c in range(3):
        g = joined(c, pl.ds(0, T))
        G[pl.ds(base_small + 8 + c, 1), pl.ds(0, WL)] = jnp.sum(g.astype(jnp.float32), axis=0, keepdims=True)
        grad = f32dot(ain[...], g, TN)
        if c < 2:
            G[pl.ds(base_pack, D), pl.ds(c * WL, WL)] = grad
        else:
            for p in range(2):
                G[pl.ds(base_pack + D, WL), pl.ds(p * WL, WL)] = grad[p * WL : (p + 1) * WL, :]
    tick()
    passed(1)

    for h in (0, 1):
        rows = pl.ds(h * half, half)
        acc = f32dot(joined(0, rows), wp[0], NT)
        for c in (1, 2):
            acc = acc + f32dot(joined(c, rows), wp[c], NT)
        PX[1, rows, :] = acc
        swap(3, h).start()

    def input_half(h, totals):
        tick(h)
        swap(3, h).wait()

        def input_rows(i, totals):
            rows = pl.ds(pl.multiple_of(h * half + i * 32, 32), 32)
            g = PX[1, rows, :] + RX[1, rows, :]
            normed, inv = norm(x[rows, :].astype(jnp.float32))
            scaled = g * ag[...]
            v = mid[rows, :] + (scaled - mean_of(scaled) - normed * mean_of(scaled * normed)) * inv
            gi[rows, :] = v.astype(jnp.bfloat16)
            return (
                totals[0] + jnp.sum(g * normed, axis=0, keepdims=True),
                totals[1] + jnp.sum(g, axis=0, keepdims=True),
            )

        return lax.fori_loop(0, half // 32, input_rows, totals)

    sums = lax.fori_loop(0, 2, input_half, (zero, zero))
    passed(2)
    small_row(0)[...] = sums[0]
    small_row(1)[...] = sums[1]
    G[pl.ds(base_small + 8, 3), pl.ds(WL, D - WL)] = jnp.zeros((3, D - WL), jnp.float32)
    G[pl.ds(base_small + 11, R - 11), :] = jnp.zeros((R - 11, D), jnp.float32)

    def body(i, carry):
        comm.step(i)
        return carry

    lax.fori_loop(at_step[0], comm.steps(), body, 0)


def unpack(moves_of, whole_ref, bo_ref, gi_ref, *refs):
    outs, local = refs[:-1], refs[-1]
    stores = []
    pairs, rows = moves_of(whole_ref, bo_ref, gi_ref, outs)
    for pair in pairs:
        cp = pltpu.make_async_copy(*pair, local.at[len(stores)])
        cp.start()
        stores.append(cp)
    for src, dst in rows:
        dst[...] = src[...]
    for cp in stores:
        cp.wait()


def unpack_moves(T, D, WL, FL, O, bo, gi, outs):
    base_out = FL + D * (FL // D)
    base_pack = base_out + WL
    base_small = base_pack + D + WL
    pairs = [(bo, outs[0]), (gi, outs[1]), (O.at[pl.ds(0, FL), :], outs[2])]
    for p in range(FL // D):
        pairs.append((O.at[pl.ds(FL + p * D, D), :], outs[3].at[:, pl.ds(p * D, D)]))
    pairs.append((O.at[pl.ds(base_out, WL), :], outs[4]))
    for c in range(2):
        pairs.append((O.at[pl.ds(base_pack, D), pl.ds(c * WL, WL)], outs[5].at[c]))
    for p in range(2):
        pairs.append((O.at[pl.ds(base_pack + D, WL), pl.ds(p * WL, WL)], outs[5].at[2, pl.ds(p * WL, WL), :]))
    rows = [(O.at[base_small + k, :], outs[6 + k]) for k in range(6)]
    for p in range(FL // D):
        rows.append((O.at[base_small + 6 + p, :], outs[12].at[pl.ds(p * D, D)]))
    rows.append((O.at[pl.ds(base_small + 8, 3), pl.ds(0, WL)], outs[13]))
    return pairs, rows


def body(
    n_dp,
    block_input,
    sequence_ids,
    attention_gain,
    attention_shift,
    packed_weight,
    packed_bias,
    output_weight,
    output_bias,
    feedforward_gain,
    feedforward_shift,
    expand_weight,
    expand_bias,
    shrink_weight,
    shrink_bias,
    grad_output,
):
    T, D = block_input.shape
    WL = packed_weight.shape[2]
    FL = shrink_weight.shape[0]
    parts = WL // LANES
    bf16, f32 = jnp.bfloat16, jnp.float32
    cosine, sine = tables(T)
    total = FL + D * (FL // D) + WL + D + WL + R

    args = [
        block_input,
        sequence_ids,
        attention_gain,
        attention_shift,
        jnp.transpose(packed_weight, (1, 0, 2)),
        packed_bias,
        output_weight,
        output_bias,
        feedforward_gain,
        feedforward_shift,
        expand_weight,
        expand_bias,
        shrink_weight,
        shrink_bias,
        grad_output,
        jnp.asarray(cosine),
        jnp.asarray(sine),
    ]
    hbm = pl.BlockSpec(memory_space=pltpu.HBM)
    vmem = pl.BlockSpec(memory_space=pltpu.VMEM)
    held = [pltpu.VMEM(a.shape, a.dtype) for i, a in enumerate(args) if i != 1]
    scratch = comm_scratch(D)
    whole, out, grad_in = pl.pallas_call(
        functools.partial(layer_kernel, n_dp),
        out_shape=[pltpu.VMEM((total, D), f32), pltpu.VMEM((T, D), bf16), pltpu.VMEM((T, D), bf16)],
        in_specs=[hbm, pl.BlockSpec(memory_space=pltpu.SMEM)] + [hbm] * 15,
        out_specs=[vmem] * 3,
        scratch_shapes=held
        + [
            pltpu.VMEM((T, D), bf16),
            pltpu.VMEM((3 * parts, T, LANES), bf16),
            pltpu.VMEM((T, WL), bf16),
            pltpu.VMEM((2 * parts, T, T), bf16),
            pltpu.VMEM((T, D), f32),
            pltpu.VMEM((T, D), bf16),
            pltpu.VMEM((T, FL), bf16),
            pltpu.VMEM((2, T, D), f32),
            pltpu.VMEM((2, T, D), f32),
            pltpu.VMEM((3 * parts, T, LANES), bf16),
            pltpu.VMEM((total, D), f32),
        ]
        + scratch[:4]
        + [pltpu.SemaphoreType.DMA((18,)), pltpu.SemaphoreType.DMA((4, 2)), pltpu.SemaphoreType.DMA((4, 2))]
        + [pltpu.SemaphoreType.DMA((T // 128,)), pltpu.SemaphoreType.DMA((T // 128,)), pltpu.VMEM((FL // WL, WL), f32)]
        + scratch[4:],
        compiler_params=pltpu.CompilerParams(
            collective_id=0, has_side_effects=True, vmem_limit_bytes=48 << 20
        ),
    )(*args)
    shapes = [
        ((T, D), bf16),
        ((T, D), bf16),
        ((FL, D), f32),
        ((D, FL), f32),
        ((WL, D), f32),
        ((3, D, WL), f32),
        *[((D,), f32)] * 6,
        ((FL,), f32),
        ((3, WL), f32),
    ]
    anywhere = pl.BlockSpec(memory_space=pl.ANY)
    got = pl.pallas_call(
        functools.partial(unpack, functools.partial(unpack_moves, T, D, WL, FL)),
        out_shape=[pltpu.HBM(*s) for s in shapes[:6]] + [jax.ShapeDtypeStruct(*s) for s in shapes[6:]],
        in_specs=[vmem] * 3,
        out_specs=[anywhere] * 6 + [vmem] * 8,
        scratch_shapes=[pltpu.SemaphoreType.DMA((32,))],
        compiler_params=pltpu.CompilerParams(vmem_limit_bytes=1 << 20),
    )(whole, out, grad_in)
    small = got[6:12]
    return (
        got[0],
        got[1],
        small[0],
        small[1],
        jnp.transpose(got[5], (1, 0, 2)),
        got[13],
        got[4],
        small[2],
        small[3],
        small[4],
        got[3],
        got[12],
        got[2],
        small[5],
    )


def solution(mesh):
    in_specs = (
        P("dp", None),
        P("dp"),
        P(),
        P(),
        P(None, None, "tensor"),
        P(None, "tensor"),
        P("tensor", None),
        P(),
        P(),
        P(),
        P(None, "tensor"),
        P("tensor"),
        P("tensor", None),
        P(),
        P("dp", None),
    )
    out_specs = (
        P("dp", None),
        P("dp", None),
        P(),
        P(),
        P(None, None, "tensor"),
        P(None, "tensor"),
        P("tensor", None),
        P(),
        P(),
        P(),
        P(None, "tensor"),
        P("tensor"),
        P("tensor", None),
        P(),
    )
    return jax.shard_map(
        functools.partial(body, mesh.shape["dp"]), mesh=mesh, in_specs=in_specs, out_specs=out_specs, check_vma=False
    )
```

```python
import functools
import math

import jax
import jax.numpy as jnp
import numpy as np
from jax import lax
from jax.experimental import pallas as pl
from jax.experimental.pallas import tpu as pltpu
from jax.sharding import PartitionSpec as P

HEAD = 64
EPSILON = 1e-05
MASKED = -1000000000.0
LANES = 128
MESH = pl.DeviceIdType.MESH
W = 4
WF = 8
R = 64
LF = 2
AHEAD = 1
SMALL = 16


class Comm:
    def __init__(self, n, counts, G, O, RF, RU, RD, RL, RS, sems):
        self.nz = n // 4
        self.counts = counts
        self.G, self.O, self.RF, self.RU, self.RD, self.RL = G, O, RF, RU, RD, RL
        self.RS = RS
        self.credits = self.nz > W
        self.sems = sems
        d = lax.axis_index("dp")
        self.t = lax.axis_index("tensor")
        self.d = d
        self.z = d // 4
        self.y = (d // 2) % 2
        self.x = d % 2
        self.px = d + 1 - 2 * self.x
        self.py = d + 2 - 4 * self.y

    def steps(self):
        return max(self.counts) + LF + 2 * self.nz

    def arrive(self):
        b = pltpu.get_barrier_semaphore()
        for peer in ((self.px, self.t), (self.py, self.t), (self.d, 1 - self.t)):
            pl.semaphore_signal(b, inc=1, device_id=peer, device_id_type=MESH)

        @pl.when(self.z > 0)
        def _():
            pl.semaphore_signal(b, inc=1, device_id=(self.d - 4, self.t), device_id_type=MESH)

        @pl.when(self.z < self.nz - 1)
        def _():
            pl.semaphore_signal(b, inc=1, device_id=(self.d + 4, self.t), device_id_type=MESH)

    def ready(self):
        edge = (self.z > 0).astype(jnp.int32) + (self.z < self.nz - 1).astype(jnp.int32)
        pl.semaphore_wait(pltpu.get_barrier_semaphore(), 3 + edge)

    def rows(self, start, size):
        return self.G.at[pl.ds(pl.multiple_of(start, 8), size), :]

    def done(self, start, size):
        return self.O.at[pl.ds(pl.multiple_of(start, 8), size), :]

    def copy(self, src, dst, kind, idx, dev):
        sent, landed = ("U" if kind == "D" else kind) + "s", ("V" if kind == "E" else kind) + "r"
        return pltpu.make_async_remote_copy(
            src_ref=src, dst_ref=dst, send_sem=self.sems[sent].at[idx], recv_sem=self.sems[landed].at[idx],
            device_id=(dev, self.t), device_id_type=MESH)

    def give(self, cond, kind, c, s, dev):
        @pl.when(cond)
        def _():
            pl.semaphore_signal(self.sems[kind].at[c, s], inc=1, device_id=(dev, self.t), device_id_type=MESH)

    def take(self, cond, kind, c, s):
        @pl.when(cond)
        def _():
            pl.semaphore_wait(self.sems[kind].at[c, s], 1)

    def add(self, start, size, buf):
        r = self.rows(start, size)
        r[...] = r[...] + buf[...]

    def step(self, i):
        for c in (0, 1):
            self.first(c, i)
        for c in (0, 1):
            self.rest(c, i)

    def base(self, c, k):
        return (2 * k + c) * R

    def small(self, i, at):
        nz, z = self.nz, self.z
        src, dst = self.rows(at, SMALL), self.done(at, SMALL)
        pairs = [self.copy(src, self.RS.at[j], "S", (j,), dev) for j, dev in ((0, self.px), (1, self.py))]
        up = self.copy(src, self.RS.at[2], "S", (2,), jnp.minimum(self.d + 4, 4 * nz - 1))
        down = self.copy(dst, dst, "S", (3,), jnp.maximum(self.d - 4, 0))

        @pl.when(i == 0)
        def _():
            pairs[0].start()

        @pl.when(i == 1)
        def _():
            pairs[0].wait()
            self.add(at, SMALL, self.RS.at[0])
            pairs[1].start()

        @pl.when(i == 2)
        def _():
            pairs[1].wait()
            self.add(at, SMALL, self.RS.at[1])

        @pl.when((i == 2 + z) & (z > 0))
        def _():
            up.wait_recv()
            self.add(at, SMALL, self.RS.at[2])

        @pl.when((i == 2 + z) & (z < nz - 1))
        def _():
            up.start()

        @pl.when((i == 3 + z) & (z < nz - 1))
        def _():
            up.wait_send()

        @pl.when((i == nz + 1) & (z == nz - 1))
        def _():
            dst[...] = src[...]

        @pl.when((i == 2 * nz - z) & (z < nz - 1))
        def _():
            down.wait_recv()

        @pl.when((i == 2 * nz - z) & (z > 0))
        def _():
            down.start()

        @pl.when((i == 2 * nz - z + 1) & (z > 0))
        def _():
            down.wait_send()

    def f_copy(self, c, k):
        a, dev = (self.x, self.px) if c == 0 else (self.y, self.py)
        q = k % WF
        return self.copy(self.rows(self.base(c, k) + (1 - a) * (R // 2), R // 2), self.RF.at[c, q], "F", (c, q), dev)

    def first(self, c, i):
        early = i < AHEAD
        k = jnp.where(early, 2 * i, i + AHEAD)

        @pl.when(k < self.counts[c])
        def _():
            self.f_copy(c, k).start()

        @pl.when(early & (2 * i + 1 < self.counts[c]))
        def _():
            self.f_copy(c, 2 * i + 1).start()

    def rest(self, c, i):
        nz, z = self.nz, self.z
        a, fdev, ldev = (self.x, self.px, self.py) if c == 0 else (self.y, self.py, self.px)
        n = self.counts[c]
        H, Q = R // 2, R // 4

        def ok(k):
            return (k >= 0) & (k < n)

        def half(k):
            return self.base(c, k) + a * H

        def sub(k, s):
            return half(k) + s * Q

        def root(k, s):
            return k % 2 if s == 0 else nz - 1 - k % 2

        k = i - LF

        @pl.when(ok(k))
        def _(k=k):
            cp = self.f_copy(c, k)
            cp.wait_send()
            cp.wait_recv()
            self.add(half(k), H, self.RF.at[c, k % WF])

        def up(k, s):
            return self.copy(self.rows(sub(k, s), Q), self.RU.at[c, s, k % W], "U", (c, s, k % W), jnp.minimum(self.d + 4, 4 * nz - 1))

        def dn(k, s):
            return self.copy(self.rows(sub(k, s), Q), self.RD.at[c, s, k % W], "D", (c, s, k % W), jnp.maximum(self.d - 4, 0))

        for s in (0, 1):
            k = i - (LF + z)

            @pl.when(ok(k) & (z <= root(k, s)) & (z > 0))
            def _(k=k, s=s):
                up(k, s).wait_recv()
                self.add(sub(k, s), Q, self.RU.at[c, s, k % W])
                if self.credits:
                    self.give(k + W < n, "CU", c, s, jnp.maximum(self.d - 4, 0))

            @pl.when(ok(k) & (z < root(k, s)))
            def _(k=k, s=s):
                if self.credits:
                    self.take(k >= W, "CU", c, s)
                up(k, s).start()

            k = i - (LF + nz - 1 - z)

            @pl.when(ok(k) & (z >= root(k, s)) & (z < nz - 1))
            def _(k=k, s=s):
                dn(k, s).wait_recv()
                self.add(sub(k, s), Q, self.RD.at[c, s, k % W])
                if self.credits:
                    self.give(k + W < n, "CD", c, s, jnp.minimum(self.d + 4, 4 * nz - 1))

            @pl.when(ok(k) & (z > root(k, s)))
            def _(k=k, s=s):
                if self.credits:
                    self.take(k >= W, "CD", c, s)
                dn(k, s).start()

            k = i - (LF + z + 1)

            @pl.when(ok(k) & (z < root(k, s)))
            def _(k=k, s=s):
                up(k, s).wait_send()

            k = i - (LF + nz - 1 - z + 1)

            @pl.when(ok(k) & (z > root(k, s)))
            def _(k=k, s=s):
                dn(k, s).wait_send()

        def cross(k, s):
            return self.copy(self.rows(sub(k, s), Q), self.RL.at[c, k % W], "L", (c, k % W), ldev)

        for s in (0, 1):
            k = i - (LF + nz - 1)

            @pl.when(ok(k) & (z == root(k, s)))
            def _(k=k, s=s):
                cross(k, s).start()

            k = i - (LF + nz)

            @pl.when(ok(k) & (z == root(k, s)))
            def _(k=k, s=s):
                cp = cross(k, s)
                cp.wait_send()
                cp.wait_recv()
                self.done(sub(k, s), Q)[...] = self.rows(sub(k, s), Q)[...] + self.RL[c, k % W]

        def g_up(k, s):
            r = self.done(sub(k, s), Q)
            return self.copy(r, r, "V", (c, s, k % W), jnp.minimum(self.d + 4, 4 * nz - 1))

        def g_dn(k, s):
            r = self.done(sub(k, s), Q)
            return self.copy(r, r, "E", (c, s, k % W), jnp.maximum(self.d - 4, 0))

        def g_first(k, s):
            r = self.done(sub(k, s), Q)
            return self.copy(r, r, "G", (c, s, k % W), fdev)

        for e in (0, 1):
            for s in (0, 1):
                r = e if s == 0 else nz - 1 - e
                lag = LF + nz + jnp.abs(z - r)
                k = i - lag
                here = ok(k) & (k % 2 == e)

                @pl.when(here & (z < r))
                def _(k=k, s=s):
                    g_dn(k, s).wait_recv()

                @pl.when(here & (z > r))
                def _(k=k, s=s):
                    g_up(k, s).wait_recv()

                @pl.when(here & (z <= r) & (z > 0))
                def _(k=k, s=s):
                    g_dn(k, s).start()

                @pl.when(here & (z >= r) & (z < nz - 1))
                def _(k=k, s=s):
                    g_up(k, s).start()

                @pl.when(here)
                def _(k=k, s=s):
                    g_first(k, s).start()

                k = i - (lag + 1)
                here = ok(k) & (k % 2 == e)

                @pl.when(here)
                def _(k=k, s=s):
                    cp = g_first(k, s)
                    cp.wait_send()
                    cp.wait_recv()

                @pl.when(here & (z <= r) & (z > 0))
                def _(k=k, s=s):
                    g_dn(k, s).wait_send()

                @pl.when(here & (z >= r) & (z < nz - 1))
                def _(k=k, s=s):
                    g_up(k, s).wait_send()


KINDS = {"F": (2, WF), "U": (2, 2, W), "D": (2, 2, W), "L": (2, W), "V": (2, 2, W), "E": (2, 2, W), "G": (2, 2, W), "S": (4,)}
SEMS = [k + e for k in KINDS for e in "sr" if k + e not in ("Ds", "Er")]
CREDITS = ["CU", "CD"]


def comm_scratch(width):
    return [
        pltpu.VMEM((2, WF, R // 2, width), jnp.float32),
        pltpu.VMEM((2, 2, W, R // 4, width), jnp.float32),
        pltpu.VMEM((2, 2, W, R // 4, width), jnp.float32),
        pltpu.VMEM((2, W, R // 4, width), jnp.float32),
        pltpu.VMEM((3, SMALL, width), jnp.float32),
    ] + [pltpu.SemaphoreType.DMA(KINDS[k[0]]) for k in SEMS] + [pltpu.SemaphoreType.REGULAR((2, 2)) for _ in CREDITS]

def f32dot(a, b, dims=((1,), (0,))):
    return lax.dot_general(a, b, (dims, ((), ())), preferred_element_type=jnp.float32)


NT = ((1,), (1,))
TN = ((0,), (0,))


def tables(tokens):
    half = HEAD // 2
    frequency = np.exp(np.arange(half) * (-2.0 * math.log(10000.0) / HEAD)).astype(np.float32)
    angles = (np.arange(tokens, dtype=np.float32)[:, None] * frequency[None, :]).astype(np.float64)
    cosine = np.tile(np.cos(angles), (1, LANES // half)).astype(np.float32)
    sign = np.where((np.arange(LANES) // half) % 2 == 0, -1.0, 1.0)
    sine = (np.tile(np.sin(angles), (1, LANES // half)) * sign).astype(np.float32)
    return cosine, sine


def swap_halves(v, low):
    return jnp.where(low, pltpu.roll(v, LANES - HEAD // 2, 1), pltpu.roll(v, HEAD // 2, 1))


def chunks(total, size, body, unroll=False):
    count = total // size

    def one(i, carry):
        body(pl.multiple_of(i * size, size))
        return carry

    lax.fori_loop(0, count, one, 0, unroll=unroll)


def mean_of(v):
    return jnp.mean(v, axis=-1, keepdims=True)


def norm(v):
    centred = v - mean_of(v)
    inv = lax.rsqrt(mean_of(centred * centred) + EPSILON)
    return centred * inv, inv


class Row:
    def __init__(self, ref):
        self.ref = ref

    def __getitem__(self, index):
        v = self.ref[...] if index is Ellipsis else self.ref[index[1]]
        return v.reshape(1, v.shape[0])


def layer_kernel(n, *refs):
    (x_h, ids_h, ag_h, as_h, wp_h, pb_h, wo_h, ob_h, fg_h, fs_h, we_h, eb_h, ws_h, sb_h, go_h, cos_h, sin_h) = refs[:17]
    O, bo, gi = refs[17:20]
    (x, ids, ag, ash, wp, pb, wo, ob, fg, fs, we, eb, ws, sb, go, cos, sin) = refs[20:37]
    ag, ash, ob, fg, fs, eb, sb = (Row(v) for v in (ag, ash, ob, fg, fs, eb, sb))
    (ain, qkv, att, prob, mid, ein, act, PX, RX, dqkv, G, RF, RU, RD, RL, RS, local, xs, xr, ys, yr, bias2) = refs[37:59]
    sems = dict(zip(SEMS + CREDITS, refs[59:]))
    T, D = x.shape
    WL = wo.shape[0]
    FL = ws.shape[0]
    half = T // 2
    parts = WL // LANES
    base_out, base_pack = FL + D * (FL // D), FL + D * (FL // D) + WL
    base_small = base_pack + D + WL
    full = base_small // (2 * R)
    comm = Comm(n, (full, full), G, O, RF, RU, RD, RL, RS, sems)
    at_step = [0]

    def tick(more=0):
        comm.step(jnp.int32(at_step[0]) + more)

    def passed(count):
        at_step[0] += count

    loads = []
    for j, (src, dst) in enumerate(
        [(x_h, x), (wp_h.at[0], wp.at[0]), (cos_h, cos), (sin_h, sin), (ag_h, ag.ref), (as_h, ash.ref), (pb_h, pb), (wo_h, wo), (ob_h, ob.ref), (fg_h, fg.ref), (fs_h, fs.ref), (we_h, we), (eb_h, eb.ref), (go_h, go), (ws_h, ws), (sb_h, sb.ref), (wp_h.at[1], wp.at[1]), (wp_h.at[2], wp.at[2]), (ids_h, ids)]
    ):
        loads.append(pltpu.make_async_copy(src, dst, local.at[j]))

    def begin(*which):
        for j in which:
            loads[j].start()

    def arrived(*which):
        for j in which:
            loads[j].wait()

    begin(0, 4, 5, 18, 1, 2, 3, 6, 16, 17)
    comm.arrive()
    arrived(0, 4, 5, 18)

    lane = lax.broadcasted_iota(jnp.int32, (1, LANES), 1)
    low_half = (lane // (HEAD // 2)) % 2 == 0
    first_head = lane < HEAD
    other = jnp.max(ids[...].reshape(1, T).astype(jnp.float32), axis=1, keepdims=True)
    col = lax.broadcasted_iota(jnp.int32, (1, T), 1)
    top_bias = jnp.where(col < half, 0.0, MASKED * other)
    low_bias = jnp.where(col < half, MASKED * other, 0.0)

    def pre_part(p):
        return G.at[pl.ds(pl.multiple_of(base_pack + p * T, 8), T), :]

    def norm_in(r):
        rows = pl.ds(r, 64)
        normed, _ = norm(x[rows, :].astype(jnp.float32))
        ain[rows, :] = (normed * ag[...] + ash[...]).astype(jnp.bfloat16)

    chunks(T, 64, norm_in)
    arrived(1, 2, 3, 6)
    begin(7, 8, 9, 10, 11, 12, 13, 14, 15)
    for table in (cos, sin):
        table[pl.ds(half, half), :] = table[pl.ds(half, half), :] * (1.0 - other) + table[pl.ds(0, half), :] * other
    tmp = PX.at[0]
    for c in range(3):
        if c > 0:
            arrived(15 + c)
        tmp[:, pl.ds(0, WL)] = f32dot(ain[...], wp[c])

        def turn(r, c=c):
            rows = pl.ds(r, 64)
            for j in range(parts):
                v = tmp[rows, pl.ds(j * LANES, LANES)] + pb[pl.ds(c, 1), pl.ds(j * LANES, LANES)]
                if c < 2:
                    v = v * cos[rows, :] + swap_halves(v, low_half) * sin[rows, :]
                if c == 0:
                    v = v.astype(jnp.bfloat16) * jnp.bfloat16(HEAD**-0.5)
                qkv[c * parts + j, rows, :] = v.astype(jnp.bfloat16)

        chunks(T, 64, turn)

    QR = 128
    blocks = T // QR

    def first_swap(i):
        rows = pl.ds(pl.multiple_of(i * QR, QR), QR)
        return pltpu.make_async_remote_copy(
            src_ref=PX.at[0, rows, :], dst_ref=RX.at[0, rows, :], send_sem=ys.at[i], recv_sem=yr.at[i],
            device_id=(comm.d, 1 - comm.t), device_id_type=MESH)

    def swap(i, h):
        rows = pl.ds(pl.multiple_of(h * half, half), half)
        return pltpu.make_async_remote_copy(
            src_ref=PX.at[i % 2, rows, :], dst_ref=RX.at[i % 2, rows, :], send_sem=xs.at[i - 1, h], recv_sem=xr.at[i - 1, h],
            device_id=(comm.d, 1 - comm.t), device_id_type=MESH)

    arrived(7, 8, 9, 10)
    comm.ready()

    def attend(i, carry):
        rows = pl.ds(pl.multiple_of(i * QR, QR), QR)
        bias = jnp.where(i < blocks // 2, top_bias, low_bias)
        scores, probs = [], []
        for j in range(parts):
            q = qkv[j, rows, :]
            zeros = jnp.zeros_like(q)
            two = jnp.concatenate([jnp.where(first_head, q, zeros), jnp.where(first_head, zeros, q)], axis=0)
            scores.append(f32dot(two, qkv[parts + j], NT) + bias)
        for j in range(parts):
            s = scores[j]
            p = jnp.exp(s - jnp.max(s, axis=-1, keepdims=True))
            p = (p * (1.0 / jnp.sum(p, axis=-1, keepdims=True))).astype(jnp.bfloat16)
            prob[2 * j, rows, :] = p[:QR]
            prob[2 * j + 1, rows, :] = p[QR:]
            probs.append(p)
        for j in range(parts):
            out = f32dot(probs[j], qkv[2 * parts + j])
            att[rows, j * LANES : (j + 1) * LANES] = jnp.where(first_head, out[:QR], out[QR:]).astype(jnp.bfloat16)
        PX[0, rows, :] = f32dot(att[rows, :], wo[...])
        first_swap(i).start()
        return carry

    lax.fori_loop(0, blocks, attend, 0)

    def middle_block(i, carry):
        first_swap(i).wait_recv()

        def middle_rows(r):
            rows = pl.ds(pl.multiple_of(i * QR + r, 64), 64)
            v = x[rows, :].astype(jnp.float32) + (PX[0, rows, :] + RX[0, rows, :]) + ob[...]
            mid[rows, :] = v
            normed, _ = norm(v)
            ein[rows, :] = (normed * fg[...] + fs[...]).astype(jnp.bfloat16)

        chunks(QR, 64, middle_rows, True)
        return carry

    lax.fori_loop(0, blocks, middle_block, 0)
    arrived(11, 12, 13)

    NB = WL
    per = D // NB

    nb = FL // NB
    for b in range(nb):
        bias2[pl.ds(b, 1), :] = eb[:, pl.ds(b * NB, NB)]

    def places(b):
        cols = pl.ds(pl.multiple_of(b * NB, LANES), NB)
        here = pl.ds(pl.multiple_of((b % per) * NB, LANES), NB)
        return cols, here, pre_part(b // per)

    def expand(b, carry):
        cols, here, pre = places(b)
        pre[:, here] = f32dot(ein[...], we[:, cols])

        def gelu_rows(r):
            rows = pl.ds(r, 64)
            v = pre[rows, here] + bias2[pl.ds(b, 1), :]
            pre[rows, here] = v
            act[rows, cols] = (v * (0.5 + 0.5 * lax.erf(v * math.sqrt(0.5)))).astype(jnp.bfloat16)

        chunks(T, 64, gelu_rows)
        G[pl.ds(pl.multiple_of(b * NB, LANES), NB), :] = f32dot(act[:, cols], go[...], TN)
        tick(b)
        return carry

    lax.fori_loop(0, nb, expand, 0)
    passed(nb)
    for i in range(blocks):
        first_swap(i).wait_send()
    arrived(14, 15)

    for h in (0, 1):
        rows = pl.ds(h * half, half)
        PX[1, rows, :] = f32dot(act[rows, :], ws[...])
        swap(1, h).start()

    def out_half(h, carry):
        tick(h)
        swap(1, h).wait()

        def out_rows(r):
            rows = pl.ds(pl.multiple_of(h * half + r, 64), 64)
            bo[rows, :] = (mid[rows, :] + (PX[1, rows, :] + RX[1, rows, :]) + sb[...]).astype(jnp.bfloat16)

        chunks(half, 64, out_rows)
        return carry

    lax.fori_loop(0, 2, out_half, 0)
    passed(2)

    def small_row(k):
        return G.at[pl.ds(base_small + k, 1), :]

    def slope(b, carry):
        cols, here, pre = places(b)
        PX[0, :, pl.ds(0, NB)] = f32dot(go[...], ws[cols, :], NT)

        def slope_rows(i, total):
            rows = pl.ds(pl.multiple_of(i * 64, 64), 64)
            v = pre[rows, here]
            slope = 0.5 + 0.5 * lax.erf(v * math.sqrt(0.5)) + v * (jnp.exp(v * v * -0.5) * (1.0 / math.sqrt(2.0 * math.pi)))
            g = (PX[0, rows, pl.ds(0, NB)] * slope).astype(jnp.bfloat16)
            act[rows, cols] = g
            return total + jnp.sum(g.astype(jnp.float32), axis=0, keepdims=True)

        bias2[pl.ds(b, 1), :] = lax.fori_loop(0, T // 64, slope_rows, jnp.zeros((1, NB), jnp.float32))
        tick(b)
        return carry

    lax.fori_loop(0, nb, slope, 0)
    passed(nb)
    for b in range(nb):
        G[pl.ds(base_small + 6 + b // per, 1), pl.ds((b % per) * NB, NB)] = bias2[pl.ds(b, 1), :]

    def expand_grad(b, carry):
        source = pl.ds(pl.multiple_of((b % per) * NB, LANES), NB)
        wide = pl.ds(pl.multiple_of((b // per) * D, LANES), D)
        G[pl.ds(pl.multiple_of(FL + b * NB, LANES), NB), :] = f32dot(ein[:, source], act[:, wide], TN)
        tick(b)
        return carry

    lax.fori_loop(0, nb, expand_grad, 0)
    passed(nb)

    for h in (0, 1):
        rows = pl.ds(h * half, half)
        PX[0, rows, :] = f32dot(act[rows, :], we[...], NT)
        swap(2, h).start()
    tick()
    passed(1)

    zero = jnp.zeros((1, D), jnp.float32)

    def back_half(h, totals):
        swap(2, h).wait()

        def back_rows(i, totals):
            rows = pl.ds(pl.multiple_of(h * half + i * 32, 32), 32)
            gain_sum, shift_sum, bias_sum, top_sum = totals
            g = PX[0, rows, :] + RX[0, rows, :]
            normed, inv = norm(mid[rows, :])
            scaled = g * fg[...]
            top = go[rows, :].astype(jnp.float32)
            gm = top + (scaled - mean_of(scaled) - normed * mean_of(scaled * normed)) * inv
            mid[rows, :] = gm
            ein[rows, :] = gm.astype(jnp.bfloat16)
            return (
                gain_sum + jnp.sum(g * normed, axis=0, keepdims=True),
                shift_sum + jnp.sum(g, axis=0, keepdims=True),
                bias_sum + jnp.sum(gm, axis=0, keepdims=True),
                top_sum + jnp.sum(top, axis=0, keepdims=True),
            )

        totals = lax.fori_loop(0, half // 32, back_rows, totals)
        tick(h)
        return totals

    sums = lax.fori_loop(0, 2, back_half, (zero, zero, zero, zero))
    passed(2)
    for k, v in zip((3, 4, 2, 5), sums):
        small_row(k)[...] = v

    G[pl.ds(base_out, WL), :] = f32dot(att[...], ein[...], TN)
    att[...] = f32dot(ein[...], wo[...], NT).astype(jnp.bfloat16)
    tick()
    passed(1)

    def attend_back(j, carry):
        keys, vals, queries = qkv[parts + j], qkv[2 * parts + j], qkv[j]
        at = pl.ds(pl.multiple_of(j * LANES, LANES), LANES)
        dv = [None, None]
        dk = [None, None]
        for r in range(0, T, QR):
            rows = pl.ds(r, QR)
            do = att[rows, at]
            q = qkv[j, rows, :]
            dq = []
            for e in (0, 1):
                dom = jnp.where(first_head if e == 0 else ~first_head, do, jnp.zeros_like(do))
                p_low = prob[2 * j + e, rows, :]
                p = p_low.astype(jnp.float32)
                dp = f32dot(dom, vals, NT)
                inner = jnp.sum(p * dp, axis=-1, keepdims=True)
                ds = (p * (dp - inner)).astype(jnp.bfloat16)
                dq.append(f32dot(ds, keys))
                add_v = f32dot(p_low, do, TN)
                add_k = f32dot(ds, q, TN)
                dv[e] = add_v if r == 0 else dv[e] + add_v
                dk[e] = add_k if r == 0 else dk[e] + add_k
            v = jnp.where(first_head, *dq) * (HEAD**-0.5)
            dqkv[j, rows, :] = (v * cos[rows, :] - swap_halves(v, low_half) * sin[rows, :]).astype(jnp.bfloat16)
            if (r // QR) % 2 == 1:
                tick(2 * j + r // (2 * QR))
        dqkv[2 * parts + j] = jnp.where(first_head, *dv).astype(jnp.bfloat16)
        v = jnp.where(first_head, *dk)
        dqkv[parts + j] = (v * cos[...] - swap_halves(v, low_half) * sin[...]).astype(jnp.bfloat16)
        return carry

    lax.fori_loop(0, parts, attend_back, 0)
    passed(2 * parts)

    def joined(c, rows):
        return jnp.concatenate([dqkv[c * parts + j, rows, :] for j in range(parts)], axis=1)

    for c in range(3):
        g = joined(c, pl.ds(0, T))
        G[pl.ds(base_small + 8 + c, 1), pl.ds(0, WL)] = jnp.sum(g.astype(jnp.float32), axis=0, keepdims=True)
        grad = f32dot(ain[...], g, TN)
        if c < 2:
            G[pl.ds(base_pack, D), pl.ds(c * WL, WL)] = grad
        else:
            for p in range(2):
                G[pl.ds(base_pack + D, WL), pl.ds(p * WL, WL)] = grad[p * WL : (p + 1) * WL, :]
    tick()
    passed(1)

    for h in (0, 1):
        rows = pl.ds(h * half, half)
        acc = f32dot(joined(0, rows), wp[0], NT)
        for c in (1, 2):
            acc = acc + f32dot(joined(c, rows), wp[c], NT)
        PX[1, rows, :] = acc
        swap(3, h).start()

    def input_half(h, totals):
        tick(h)
        swap(3, h).wait()

        def input_rows(i, totals):
            rows = pl.ds(pl.multiple_of(h * half + i * 32, 32), 32)
            g = PX[1, rows, :] + RX[1, rows, :]
            normed, inv = norm(x[rows, :].astype(jnp.float32))
            scaled = g * ag[...]
            v = mid[rows, :] + (scaled - mean_of(scaled) - normed * mean_of(scaled * normed)) * inv
            gi[rows, :] = v.astype(jnp.bfloat16)
            return (
                totals[0] + jnp.sum(g * normed, axis=0, keepdims=True),
                totals[1] + jnp.sum(g, axis=0, keepdims=True),
            )

        return lax.fori_loop(0, half // 32, input_rows, totals)

    sums = lax.fori_loop(0, 2, input_half, (zero, zero))
    passed(2)
    small_row(0)[...] = sums[0]
    small_row(1)[...] = sums[1]
    G[pl.ds(base_small + 8, 3), pl.ds(WL, D - WL)] = jnp.zeros((3, D - WL), jnp.float32)
    G[pl.ds(base_small + 11, SMALL - 11), :] = jnp.zeros((SMALL - 11, D), jnp.float32)

    def body(i, carry):
        comm.step(i)
        comm.small(i - at_step[0], base_small)
        return carry

    lax.fori_loop(at_step[0], comm.steps(), body, 0)


def unpack(moves_of, whole_ref, bo_ref, gi_ref, *refs):
    outs, local = refs[:-1], refs[-1]
    stores = []
    pairs, rows = moves_of(whole_ref, bo_ref, gi_ref, outs)
    for pair in pairs:
        cp = pltpu.make_async_copy(*pair, local.at[len(stores)])
        cp.start()
        stores.append(cp)
    for src, dst in rows:
        dst[...] = src[...]
    for cp in stores:
        cp.wait()


def unpack_moves(T, D, WL, FL, O, bo, gi, outs):
    base_out = FL + D * (FL // D)
    base_pack = base_out + WL
    base_small = base_pack + D + WL
    pairs = [(bo, outs[0]), (gi, outs[1]), (O.at[pl.ds(0, FL), :], outs[2])]
    for p in range(FL // D):
        pairs.append((O.at[pl.ds(FL + p * D, D), :], outs[3].at[:, pl.ds(p * D, D)]))
    pairs.append((O.at[pl.ds(base_out, WL), :], outs[4]))
    for c in range(2):
        pairs.append((O.at[pl.ds(base_pack, D), pl.ds(c * WL, WL)], outs[5].at[c]))
    for p in range(2):
        pairs.append((O.at[pl.ds(base_pack + D, WL), pl.ds(p * WL, WL)], outs[5].at[2, pl.ds(p * WL, WL), :]))
    rows = [(O.at[base_small + k, :], outs[6 + k]) for k in range(6)]
    for p in range(FL // D):
        rows.append((O.at[base_small + 6 + p, :], outs[12].at[pl.ds(p * D, D)]))
    rows.append((O.at[pl.ds(base_small + 8, 3), pl.ds(0, WL)], outs[13]))
    return pairs, rows


def body(
    n_dp,
    block_input,
    sequence_ids,
    attention_gain,
    attention_shift,
    packed_weight,
    packed_bias,
    output_weight,
    output_bias,
    feedforward_gain,
    feedforward_shift,
    expand_weight,
    expand_bias,
    shrink_weight,
    shrink_bias,
    grad_output,
):
    T, D = block_input.shape
    WL = packed_weight.shape[2]
    FL = shrink_weight.shape[0]
    parts = WL // LANES
    bf16, f32 = jnp.bfloat16, jnp.float32
    cosine, sine = tables(T)
    total = FL + D * (FL // D) + WL + D + WL + SMALL

    args = [
        block_input,
        sequence_ids,
        attention_gain,
        attention_shift,
        jnp.transpose(packed_weight, (1, 0, 2)),
        packed_bias,
        output_weight,
        output_bias,
        feedforward_gain,
        feedforward_shift,
        expand_weight,
        expand_bias,
        shrink_weight,
        shrink_bias,
        grad_output,
        jnp.asarray(cosine),
        jnp.asarray(sine),
    ]
    hbm = pl.BlockSpec(memory_space=pltpu.HBM)
    vmem = pl.BlockSpec(memory_space=pltpu.VMEM)
    held = [pltpu.VMEM(a.shape, a.dtype) for a in args]
    scratch = comm_scratch(D)
    whole, out, grad_in = pl.pallas_call(
        functools.partial(layer_kernel, n_dp),
        out_shape=[pltpu.VMEM((total, D), f32), pltpu.VMEM((T, D), bf16), pltpu.VMEM((T, D), bf16)],
        in_specs=[hbm] * 17,
        out_specs=[vmem] * 3,
        scratch_shapes=held
        + [
            pltpu.VMEM((T, D), bf16),
            pltpu.VMEM((3 * parts, T, LANES), bf16),
            pltpu.VMEM((T, WL), bf16),
            pltpu.VMEM((2 * parts, T, T), bf16),
            pltpu.VMEM((T, D), f32),
            pltpu.VMEM((T, D), bf16),
            pltpu.VMEM((T, FL), bf16),
            pltpu.VMEM((2, T, D), f32),
            pltpu.VMEM((2, T, D), f32),
            pltpu.VMEM((3 * parts, T, LANES), bf16),
            pltpu.VMEM((total, D), f32),
        ]
        + scratch[:5]
        + [pltpu.SemaphoreType.DMA((19,)), pltpu.SemaphoreType.DMA((3, 2)), pltpu.SemaphoreType.DMA((3, 2))]
        + [pltpu.SemaphoreType.DMA((T // 128,)), pltpu.SemaphoreType.DMA((T // 128,)), pltpu.VMEM((FL // WL, WL), f32)]
        + scratch[5:],
        compiler_params=pltpu.CompilerParams(
            collective_id=0, has_side_effects=True, vmem_limit_bytes=48 << 20
        ),
    )(*args)
    shapes = [
        ((T, D), bf16),
        ((T, D), bf16),
        ((FL, D), f32),
        ((D, FL), f32),
        ((WL, D), f32),
        ((3, D, WL), f32),
        *[((D,), f32)] * 6,
        ((FL,), f32),
        ((3, WL), f32),
    ]
    anywhere = pl.BlockSpec(memory_space=pl.ANY)
    got = pl.pallas_call(
        functools.partial(unpack, functools.partial(unpack_moves, T, D, WL, FL)),
        out_shape=[pltpu.HBM(*s) for s in shapes[:6]] + [jax.ShapeDtypeStruct(*s) for s in shapes[6:]],
        in_specs=[vmem] * 3,
        out_specs=[anywhere] * 6 + [vmem] * 8,
        scratch_shapes=[pltpu.SemaphoreType.DMA((32,))],
        compiler_params=pltpu.CompilerParams(vmem_limit_bytes=1 << 20),
    )(whole, out, grad_in)
    small = got[6:12]
    return (
        got[0],
        got[1],
        small[0],
        small[1],
        jnp.transpose(got[5], (1, 0, 2)),
        got[13],
        got[4],
        small[2],
        small[3],
        small[4],
        got[3],
        got[12],
        got[2],
        small[5],
    )


def solution(mesh):
    in_specs = (
        P("dp", None),
        P("dp"),
        P(),
        P(),
        P(None, None, "tensor"),
        P(None, "tensor"),
        P("tensor", None),
        P(),
        P(),
        P(),
        P(None, "tensor"),
        P("tensor"),
        P("tensor", None),
        P(),
        P("dp", None),
    )
    out_specs = (
        P("dp", None),
        P("dp", None),
        P(),
        P(),
        P(None, None, "tensor"),
        P(None, "tensor"),
        P("tensor", None),
        P(),
        P(),
        P(),
        P(None, "tensor"),
        P("tensor"),
        P("tensor", None),
        P(),
    )
    return jax.shard_map(
        functools.partial(body, mesh.shape["dp"]), mesh=mesh, in_specs=in_specs, out_specs=out_specs, check_vma=False
    )
```

```python
import functools
import math

import jax
import jax.numpy as jnp
import numpy as np
from jax import lax
from jax.experimental import pallas as pl
from jax.experimental.pallas import tpu as pltpu
from jax.sharding import PartitionSpec as P

HEAD = 64
EPSILON = 1e-05
MASKED = -1000000000.0
LANES = 128
MESH = pl.DeviceIdType.MESH
W = 4
WF = 8
R = 64
LF = 2
AHEAD = 1
SMALL = 16


class Comm:
    def __init__(self, n, counts, G, O, RF, RU, RD, RL, RS, sems):
        self.nz = n // 4
        self.counts = counts
        self.G, self.O, self.RF, self.RU, self.RD, self.RL = G, O, RF, RU, RD, RL
        self.RS = RS
        self.credits = self.nz > W
        self.sems = sems
        d = lax.axis_index("dp")
        self.t = lax.axis_index("tensor")
        self.d = d
        self.z = d // 4
        self.y = (d // 2) % 2
        self.x = d % 2
        self.px = d + 1 - 2 * self.x
        self.py = d + 2 - 4 * self.y

    def steps(self):
        return max(self.counts) + LF + 2 * self.nz

    def arrive(self):
        b = pltpu.get_barrier_semaphore()
        for peer in ((self.px, self.t), (self.py, self.t), (self.d, 1 - self.t)):
            pl.semaphore_signal(b, inc=1, device_id=peer, device_id_type=MESH)

        @pl.when(self.z > 0)
        def _():
            pl.semaphore_signal(b, inc=1, device_id=(self.d - 4, self.t), device_id_type=MESH)

        @pl.when(self.z < self.nz - 1)
        def _():
            pl.semaphore_signal(b, inc=1, device_id=(self.d + 4, self.t), device_id_type=MESH)

    def ready(self):
        edge = (self.z > 0).astype(jnp.int32) + (self.z < self.nz - 1).astype(jnp.int32)
        pl.semaphore_wait(pltpu.get_barrier_semaphore(), 3 + edge)

    def rows(self, start, size):
        return self.G.at[pl.ds(pl.multiple_of(start, 8), size), :]

    def done(self, start, size):
        return self.O.at[pl.ds(pl.multiple_of(start, 8), size), :]

    def copy(self, src, dst, kind, idx, dev):
        sent, landed = ("U" if kind == "D" else kind) + "s", ("V" if kind == "E" else kind) + "r"
        return pltpu.make_async_remote_copy(
            src_ref=src, dst_ref=dst, send_sem=self.sems[sent].at[idx], recv_sem=self.sems[landed].at[idx],
            device_id=(dev, self.t), device_id_type=MESH)

    def give(self, cond, kind, c, s, dev):
        @pl.when(cond)
        def _():
            pl.semaphore_signal(self.sems[kind].at[c, s], inc=1, device_id=(dev, self.t), device_id_type=MESH)

    def take(self, cond, kind, c, s):
        @pl.when(cond)
        def _():
            pl.semaphore_wait(self.sems[kind].at[c, s], 1)

    def add(self, start, size, buf):
        r = self.rows(start, size)
        r[...] = r[...] + buf[...]

    def step(self, i):
        for c in (0, 1):
            self.first(c, i)
        for c in (0, 1):
            self.rest(c, i)

    def base(self, c, k):
        return (2 * k + c) * R

    def small(self, i, at):
        nz, z = self.nz, self.z
        src, dst = self.rows(at, SMALL), self.done(at, SMALL)
        pairs = [self.copy(src, self.RS.at[j], "S", (j,), dev) for j, dev in ((0, self.px), (1, self.py))]
        up = self.copy(src, self.RS.at[2], "S", (2,), jnp.minimum(self.d + 4, 4 * nz - 1))
        down = self.copy(dst, dst, "S", (3,), jnp.maximum(self.d - 4, 0))

        @pl.when(i == 0)
        def _():
            pairs[0].start()

        @pl.when(i == 1)
        def _():
            pairs[0].wait()
            self.add(at, SMALL, self.RS.at[0])
            pairs[1].start()

        @pl.when(i == 2)
        def _():
            pairs[1].wait()
            self.add(at, SMALL, self.RS.at[1])

        @pl.when((i == 2 + z) & (z > 0))
        def _():
            up.wait_recv()
            self.add(at, SMALL, self.RS.at[2])

        @pl.when((i == 2 + z) & (z < nz - 1))
        def _():
            up.start()

        @pl.when((i == 3 + z) & (z < nz - 1))
        def _():
            up.wait_send()

        @pl.when((i == nz + 1) & (z == nz - 1))
        def _():
            dst[...] = src[...]

        @pl.when((i == 2 * nz - z) & (z < nz - 1))
        def _():
            down.wait_recv()

        @pl.when((i == 2 * nz - z) & (z > 0))
        def _():
            down.start()

        @pl.when((i == 2 * nz - z + 1) & (z > 0))
        def _():
            down.wait_send()

    def f_copy(self, c, k):
        a, dev = (self.x, self.px) if c == 0 else (self.y, self.py)
        q = k % WF
        return self.copy(self.rows(self.base(c, k) + (1 - a) * (R // 2), R // 2), self.RF.at[c, q], "F", (c, q), dev)

    def first(self, c, i):
        early = i < AHEAD
        k = jnp.where(early, 2 * i, i + AHEAD)

        @pl.when(k < self.counts[c])
        def _():
            self.f_copy(c, k).start()

        @pl.when(early & (2 * i + 1 < self.counts[c]))
        def _():
            self.f_copy(c, 2 * i + 1).start()

    def rest(self, c, i):
        nz, z = self.nz, self.z
        a, fdev, ldev = (self.x, self.px, self.py) if c == 0 else (self.y, self.py, self.px)
        n = self.counts[c]
        H, Q = R // 2, R // 4

        def ok(k):
            return (k >= 0) & (k < n)

        def half(k):
            return self.base(c, k) + a * H

        def sub(k, s):
            return half(k) + s * Q

        def root(k, s):
            return k % 2 if s == 0 else nz - 1 - k % 2

        k = i - LF

        @pl.when(ok(k))
        def _(k=k):
            cp = self.f_copy(c, k)
            cp.wait_send()
            cp.wait_recv()
            self.add(half(k), H, self.RF.at[c, k % WF])

        def up(k, s):
            return self.copy(self.rows(sub(k, s), Q), self.RU.at[c, s, k % W], "U", (c, s, k % W), jnp.minimum(self.d + 4, 4 * nz - 1))

        def dn(k, s):
            return self.copy(self.rows(sub(k, s), Q), self.RD.at[c, s, k % W], "D", (c, s, k % W), jnp.maximum(self.d - 4, 0))

        for s in (0, 1):
            k = i - (LF + z)

            @pl.when(ok(k) & (z <= root(k, s)) & (z > 0))
            def _(k=k, s=s):
                up(k, s).wait_recv()
                self.add(sub(k, s), Q, self.RU.at[c, s, k % W])
                if self.credits:
                    self.give(k + W < n, "CU", c, s, jnp.maximum(self.d - 4, 0))

            @pl.when(ok(k) & (z < root(k, s)))
            def _(k=k, s=s):
                if self.credits:
                    self.take(k >= W, "CU", c, s)
                up(k, s).start()

            k = i - (LF + nz - 1 - z)

            @pl.when(ok(k) & (z >= root(k, s)) & (z < nz - 1))
            def _(k=k, s=s):
                dn(k, s).wait_recv()
                self.add(sub(k, s), Q, self.RD.at[c, s, k % W])
                if self.credits:
                    self.give(k + W < n, "CD", c, s, jnp.minimum(self.d + 4, 4 * nz - 1))

            @pl.when(ok(k) & (z > root(k, s)))
            def _(k=k, s=s):
                if self.credits:
                    self.take(k >= W, "CD", c, s)
                dn(k, s).start()

            k = i - (LF + z + 1)

            @pl.when(ok(k) & (z < root(k, s)))
            def _(k=k, s=s):
                up(k, s).wait_send()

            k = i - (LF + nz - 1 - z + 1)

            @pl.when(ok(k) & (z > root(k, s)))
            def _(k=k, s=s):
                dn(k, s).wait_send()

        def cross(k, s):
            return self.copy(self.rows(sub(k, s), Q), self.RL.at[c, k % W], "L", (c, k % W), ldev)

        for s in (0, 1):
            k = i - (LF + nz - 1)

            @pl.when(ok(k) & (z == root(k, s)))
            def _(k=k, s=s):
                cross(k, s).start()

            k = i - (LF + nz)

            @pl.when(ok(k) & (z == root(k, s)))
            def _(k=k, s=s):
                cp = cross(k, s)
                cp.wait_send()
                cp.wait_recv()
                self.done(sub(k, s), Q)[...] = self.rows(sub(k, s), Q)[...] + self.RL[c, k % W]

        def g_up(k, s):
            r = self.done(sub(k, s), Q)
            return self.copy(r, r, "V", (c, s, k % W), jnp.minimum(self.d + 4, 4 * nz - 1))

        def g_dn(k, s):
            r = self.done(sub(k, s), Q)
            return self.copy(r, r, "E", (c, s, k % W), jnp.maximum(self.d - 4, 0))

        def g_first(k, s):
            r = self.done(sub(k, s), Q)
            return self.copy(r, r, "G", (c, s, k % W), fdev)

        for e in (0, 1):
            for s in (0, 1):
                r = e if s == 0 else nz - 1 - e
                lag = LF + nz + jnp.abs(z - r)
                k = i - lag
                here = ok(k) & (k % 2 == e)

                @pl.when(here & (z < r))
                def _(k=k, s=s):
                    g_dn(k, s).wait_recv()

                @pl.when(here & (z > r))
                def _(k=k, s=s):
                    g_up(k, s).wait_recv()

                @pl.when(here & (z <= r) & (z > 0))
                def _(k=k, s=s):
                    g_dn(k, s).start()

                @pl.when(here & (z >= r) & (z < nz - 1))
                def _(k=k, s=s):
                    g_up(k, s).start()

                @pl.when(here)
                def _(k=k, s=s):
                    g_first(k, s).start()

                k = i - (lag + 1)
                here = ok(k) & (k % 2 == e)

                @pl.when(here)
                def _(k=k, s=s):
                    cp = g_first(k, s)
                    cp.wait_send()
                    cp.wait_recv()

                @pl.when(here & (z <= r) & (z > 0))
                def _(k=k, s=s):
                    g_dn(k, s).wait_send()

                @pl.when(here & (z >= r) & (z < nz - 1))
                def _(k=k, s=s):
                    g_up(k, s).wait_send()


KINDS = {"F": (2, WF), "U": (2, 2, W), "D": (2, 2, W), "L": (2, W), "V": (2, 2, W), "E": (2, 2, W), "G": (2, 2, W), "S": (4,)}
SEMS = [k + e for k in KINDS for e in "sr" if k + e not in ("Ds", "Er")]
CREDITS = ["CU", "CD"]


def comm_scratch(width):
    return [
        pltpu.VMEM((2, WF, R // 2, width), jnp.float32),
        pltpu.VMEM((2, 2, W, R // 4, width), jnp.float32),
        pltpu.VMEM((2, 2, W, R // 4, width), jnp.float32),
        pltpu.VMEM((2, W, R // 4, width), jnp.float32),
        pltpu.VMEM((3, SMALL, width), jnp.float32),
    ] + [pltpu.SemaphoreType.DMA(KINDS[k[0]]) for k in SEMS] + [pltpu.SemaphoreType.REGULAR((2, 2)) for _ in CREDITS]

def f32dot(a, b, dims=((1,), (0,))):
    return lax.dot_general(a, b, (dims, ((), ())), preferred_element_type=jnp.float32)


NT = ((1,), (1,))
TN = ((0,), (0,))


def tables(tokens):
    half = HEAD // 2
    frequency = np.exp(np.arange(half) * (-2.0 * math.log(10000.0) / HEAD)).astype(np.float32)
    angles = (np.arange(tokens, dtype=np.float32)[:, None] * frequency[None, :]).astype(np.float64)
    cosine = np.tile(np.cos(angles), (1, LANES // half)).astype(np.float32)
    sign = np.where((np.arange(LANES) // half) % 2 == 0, -1.0, 1.0)
    sine = (np.tile(np.sin(angles), (1, LANES // half)) * sign).astype(np.float32)
    return cosine, sine


def swap_halves(v, low):
    return jnp.where(low, pltpu.roll(v, LANES - HEAD // 2, 1), pltpu.roll(v, HEAD // 2, 1))


def chunks(total, size, body, unroll=False):
    count = total // size

    def one(i, carry):
        body(pl.multiple_of(i * size, size))
        return carry

    lax.fori_loop(0, count, one, 0, unroll=unroll)


def mean_of(v):
    return jnp.mean(v, axis=-1, keepdims=True)


def norm(v):
    centred = v - mean_of(v)
    inv = lax.rsqrt(mean_of(centred * centred) + EPSILON)
    return centred * inv, inv


class Row:
    def __init__(self, ref):
        self.ref = ref

    def __getitem__(self, index):
        v = self.ref[...] if index is Ellipsis else self.ref[index[1]]
        return v.reshape(1, v.shape[0])


def layer_kernel(n, *refs):
    (x_h, ids_h, ag_h, as_h, wp_h, pb_h, wo_h, ob_h, fg_h, fs_h, we_h, eb_h, ws_h, sb_h, go_h, cos_h, sin_h) = refs[:17]
    O, bo, gi = refs[17:20]
    (x, ids, ag, ash, wp, pb, wo, ob, fg, fs, we, eb, ws, sb, go, cos, sin) = refs[20:37]
    ag, ash, ob, fg, fs, eb, sb = (Row(v) for v in (ag, ash, ob, fg, fs, eb, sb))
    (ain, qkv, att, prob, mid, ein, act, PX, RX, dqkv, G, RF, RU, RD, RL, RS, local, xs, xr, ys, yr, bias2) = refs[37:59]
    sems = dict(zip(SEMS + CREDITS, refs[59:]))
    T, D = x.shape
    WL = wo.shape[0]
    FL = ws.shape[0]
    half = T // 2
    parts = WL // LANES
    base_out, base_pack = FL + D * (FL // D), FL + D * (FL // D) + WL
    base_small = base_pack + D + WL
    full = base_small // (2 * R)
    comm = Comm(n, (full, full), G, O, RF, RU, RD, RL, RS, sems)
    at_step = [0]

    def tick(more=0):
        comm.step(jnp.int32(at_step[0]) + more)

    def passed(count):
        at_step[0] += count

    loads = []
    for j, (src, dst) in enumerate(
        [(x_h, x), (wp_h.at[0], wp.at[0]), (cos_h, cos), (sin_h, sin), (ag_h, ag.ref), (as_h, ash.ref), (pb_h, pb), (wo_h, wo), (ob_h, ob.ref), (fg_h, fg.ref), (fs_h, fs.ref), (we_h, we), (eb_h, eb.ref), (go_h, go), (ws_h, ws), (sb_h, sb.ref), (wp_h.at[1], wp.at[1]), (wp_h.at[2], wp.at[2]), (ids_h, ids)]
    ):
        loads.append(pltpu.make_async_copy(src, dst, local.at[j]))

    def begin(*which):
        for j in which:
            loads[j].start()

    def arrived(*which):
        for j in which:
            loads[j].wait()

    begin(0, 4, 5, 18, 1, 2, 3, 6, 16, 17)
    comm.arrive()
    arrived(0, 4, 5, 18)

    lane = lax.broadcasted_iota(jnp.int32, (1, LANES), 1)
    low_half = (lane // (HEAD // 2)) % 2 == 0
    first_head = lane < HEAD
    other = jnp.max(ids[...].reshape(1, T).astype(jnp.float32), axis=1, keepdims=True)
    col = lax.broadcasted_iota(jnp.int32, (1, T), 1)
    top_bias = jnp.where(col < half, 0.0, MASKED * other)
    low_bias = jnp.where(col < half, MASKED * other, 0.0)

    def pre_part(p):
        return G.at[pl.ds(pl.multiple_of(base_pack + p * T, 8), T), :]

    def norm_in(r):
        rows = pl.ds(r, 64)
        normed, _ = norm(x[rows, :].astype(jnp.float32))
        ain[rows, :] = (normed * ag[...] + ash[...]).astype(jnp.bfloat16)

    chunks(T, 64, norm_in, True)
    arrived(1, 2, 3, 6)
    begin(7, 8, 9, 10, 11, 12, 13, 14, 15)
    for table in (cos, sin):
        table[pl.ds(half, half), :] = table[pl.ds(half, half), :] * (1.0 - other) + table[pl.ds(0, half), :] * other
    tmp = PX.at[0]
    for c in range(3):
        if c > 0:
            arrived(15 + c)
        tmp[:, pl.ds(0, WL)] = f32dot(ain[...], wp[c])

        def turn(r, c=c):
            rows = pl.ds(r, 64)
            for j in range(parts):
                v = tmp[rows, pl.ds(j * LANES, LANES)] + pb[pl.ds(c, 1), pl.ds(j * LANES, LANES)]
                if c < 2:
                    v = v * cos[rows, :] + swap_halves(v, low_half) * sin[rows, :]
                if c == 0:
                    v = v.astype(jnp.bfloat16) * jnp.bfloat16(HEAD**-0.5)
                qkv[c * parts + j, rows, :] = v.astype(jnp.bfloat16)

        chunks(T, 64, turn, True)

    QR = 256
    blocks = T // QR

    def first_swap(i):
        rows = pl.ds(pl.multiple_of(i * QR, QR), QR)
        return pltpu.make_async_remote_copy(
            src_ref=PX.at[0, rows, :], dst_ref=RX.at[0, rows, :], send_sem=ys.at[i], recv_sem=yr.at[i],
            device_id=(comm.d, 1 - comm.t), device_id_type=MESH)

    def swap(i, h):
        rows = pl.ds(pl.multiple_of(h * half, half), half)
        return pltpu.make_async_remote_copy(
            src_ref=PX.at[i % 2, rows, :], dst_ref=RX.at[i % 2, rows, :], send_sem=xs.at[i - 1, h], recv_sem=xr.at[i - 1, h],
            device_id=(comm.d, 1 - comm.t), device_id_type=MESH)

    arrived(7, 8, 9, 10)
    comm.ready()

    def attend(i, carry):
        rows = pl.ds(pl.multiple_of(i * QR, QR), QR)
        bias = jnp.where(i < blocks // 2, top_bias, low_bias)
        scores, probs = [], []
        for j in range(parts):
            q = qkv[j, rows, :]
            zeros = jnp.zeros_like(q)
            two = jnp.concatenate([jnp.where(first_head, q, zeros), jnp.where(first_head, zeros, q)], axis=0)
            scores.append(f32dot(two, qkv[parts + j], NT) + bias)
        for j in range(parts):
            s = scores[j]
            p = jnp.exp(s - jnp.max(s, axis=-1, keepdims=True))
            p = (p * (1.0 / jnp.sum(p, axis=-1, keepdims=True))).astype(jnp.bfloat16)
            prob[2 * j, rows, :] = p[:QR]
            prob[2 * j + 1, rows, :] = p[QR:]
            probs.append(p)
        for j in range(parts):
            out = f32dot(probs[j], qkv[2 * parts + j])
            att[rows, j * LANES : (j + 1) * LANES] = jnp.where(first_head, out[:QR], out[QR:]).astype(jnp.bfloat16)
        PX[0, rows, :] = f32dot(att[rows, :], wo[...])
        first_swap(i).start()
        return carry

    lax.fori_loop(0, blocks, attend, 0)

    def middle_block(i, carry):
        first_swap(i).wait_recv()

        def middle_rows(r):
            rows = pl.ds(pl.multiple_of(i * QR + r, 64), 64)
            v = x[rows, :].astype(jnp.float32) + (PX[0, rows, :] + RX[0, rows, :]) + ob[...]
            mid[rows, :] = v
            normed, _ = norm(v)
            ein[rows, :] = (normed * fg[...] + fs[...]).astype(jnp.bfloat16)

        chunks(QR, 64, middle_rows, True)
        return carry

    lax.fori_loop(0, blocks, middle_block, 0)
    arrived(11, 12, 13)

    NB = WL
    per = D // NB

    nb = FL // NB
    for b in range(nb):
        bias2[pl.ds(b, 1), :] = eb[:, pl.ds(b * NB, NB)]

    def places(b):
        cols = pl.ds(pl.multiple_of(b * NB, LANES), NB)
        here = pl.ds(pl.multiple_of((b % per) * NB, LANES), NB)
        return cols, here, pre_part(b // per)

    def expand(b, carry):
        cols, here, pre = places(b)
        pre[:, here] = f32dot(ein[...], we[:, cols])

        def gelu_rows(r):
            rows = pl.ds(r, 64)
            v = pre[rows, here] + bias2[pl.ds(b, 1), :]
            pre[rows, here] = v
            act[rows, cols] = (v * (0.5 + 0.5 * lax.erf(v * math.sqrt(0.5)))).astype(jnp.bfloat16)

        chunks(T, 64, gelu_rows, True)
        G[pl.ds(pl.multiple_of(b * NB, LANES), NB), :] = f32dot(act[:, cols], go[...], TN)
        tick(b)
        return carry

    lax.fori_loop(0, nb, expand, 0)
    passed(nb)
    for i in range(blocks):
        first_swap(i).wait_send()
    arrived(14, 15)

    for h in (0, 1):
        rows = pl.ds(h * half, half)
        PX[1, rows, :] = f32dot(act[rows, :], ws[...])
        swap(1, h).start()

    def out_half(h, carry):
        tick(h)
        swap(1, h).wait()

        def out_rows(r):
            rows = pl.ds(pl.multiple_of(h * half + r, 64), 64)
            bo[rows, :] = (mid[rows, :] + (PX[1, rows, :] + RX[1, rows, :]) + sb[...]).astype(jnp.bfloat16)

        chunks(half, 64, out_rows)
        return carry

    lax.fori_loop(0, 2, out_half, 0)
    passed(2)

    def small_row(k):
        return G.at[pl.ds(base_small + k, 1), :]

    def slope(b, carry):
        cols, here, pre = places(b)
        PX[0, :, pl.ds(0, NB)] = f32dot(go[...], ws[cols, :], NT)

        def slope_rows(i, total):
            rows = pl.ds(pl.multiple_of(i * 64, 64), 64)
            v = pre[rows, here]
            slope = 0.5 + 0.5 * lax.erf(v * math.sqrt(0.5)) + v * (jnp.exp(v * v * -0.5) * (1.0 / math.sqrt(2.0 * math.pi)))
            g = (PX[0, rows, pl.ds(0, NB)] * slope).astype(jnp.bfloat16)
            act[rows, cols] = g
            return total + jnp.sum(g.astype(jnp.float32), axis=0, keepdims=True)

        bias2[pl.ds(b, 1), :] = lax.fori_loop(0, T // 64, slope_rows, jnp.zeros((1, NB), jnp.float32))
        tick(b)
        return carry

    lax.fori_loop(0, nb, slope, 0)
    passed(nb)
    for b in range(nb):
        G[pl.ds(base_small + 6 + b // per, 1), pl.ds((b % per) * NB, NB)] = bias2[pl.ds(b, 1), :]

    def expand_grad(b, carry):
        source = pl.ds(pl.multiple_of((b % per) * NB, LANES), NB)
        wide = pl.ds(pl.multiple_of((b // per) * D, LANES), D)
        G[pl.ds(pl.multiple_of(FL + b * NB, LANES), NB), :] = f32dot(ein[:, source], act[:, wide], TN)
        tick(b)
        return carry

    lax.fori_loop(0, nb, expand_grad, 0)
    passed(nb)

    for h in (0, 1):
        rows = pl.ds(h * half, half)
        PX[0, rows, :] = f32dot(act[rows, :], we[...], NT)
        swap(2, h).start()
    tick()
    passed(1)

    zero = jnp.zeros((1, D), jnp.float32)

    def back_half(h, totals):
        swap(2, h).wait()

        def back_rows(i, totals):
            rows = pl.ds(pl.multiple_of(h * half + i * 32, 32), 32)
            gain_sum, shift_sum, bias_sum, top_sum = totals
            g = PX[0, rows, :] + RX[0, rows, :]
            normed, inv = norm(mid[rows, :])
            scaled = g * fg[...]
            top = go[rows, :].astype(jnp.float32)
            gm = top + (scaled - mean_of(scaled) - normed * mean_of(scaled * normed)) * inv
            mid[rows, :] = gm
            ein[rows, :] = gm.astype(jnp.bfloat16)
            return (
                gain_sum + jnp.sum(g * normed, axis=0, keepdims=True),
                shift_sum + jnp.sum(g, axis=0, keepdims=True),
                bias_sum + jnp.sum(gm, axis=0, keepdims=True),
                top_sum + jnp.sum(top, axis=0, keepdims=True),
            )

        totals = lax.fori_loop(0, half // 32, back_rows, totals)
        tick(h)
        return totals

    sums = lax.fori_loop(0, 2, back_half, (zero, zero, zero, zero))
    passed(2)
    for k, v in zip((3, 4, 2, 5), sums):
        small_row(k)[...] = v

    G[pl.ds(base_out, WL), :] = f32dot(att[...], ein[...], TN)
    att[...] = f32dot(ein[...], wo[...], NT).astype(jnp.bfloat16)
    tick()
    passed(1)

    def attend_back(j, carry):
        keys, vals, queries = qkv[parts + j], qkv[2 * parts + j], qkv[j]
        at = pl.ds(pl.multiple_of(j * LANES, LANES), LANES)
        dv = [None, None]
        dk = [None, None]
        for r in range(0, T, 128):
            rows = pl.ds(r, 128)
            do = att[rows, at]
            q = qkv[j, rows, :]
            dq = []
            for e in (0, 1):
                dom = jnp.where(first_head if e == 0 else ~first_head, do, jnp.zeros_like(do))
                p_low = prob[2 * j + e, rows, :]
                p = p_low.astype(jnp.float32)
                dp = f32dot(dom, vals, NT)
                inner = jnp.sum(p * dp, axis=-1, keepdims=True)
                ds = (p * (dp - inner)).astype(jnp.bfloat16)
                dq.append(f32dot(ds, keys))
                add_v = f32dot(p_low, do, TN)
                add_k = f32dot(ds, q, TN)
                dv[e] = add_v if r == 0 else dv[e] + add_v
                dk[e] = add_k if r == 0 else dk[e] + add_k
            v = jnp.where(first_head, *dq) * (HEAD**-0.5)
            dqkv[j, rows, :] = (v * cos[rows, :] - swap_halves(v, low_half) * sin[rows, :]).astype(jnp.bfloat16)
            if (r // 128) % 2 == 1:
                tick(2 * j + r // (2 * 128))
        dqkv[2 * parts + j] = jnp.where(first_head, *dv).astype(jnp.bfloat16)
        v = jnp.where(first_head, *dk)
        dqkv[parts + j] = (v * cos[...] - swap_halves(v, low_half) * sin[...]).astype(jnp.bfloat16)
        return carry

    lax.fori_loop(0, parts, attend_back, 0)
    passed(2 * parts)

    def joined(c, rows):
        return jnp.concatenate([dqkv[c * parts + j, rows, :] for j in range(parts)], axis=1)

    for c in range(3):
        g = joined(c, pl.ds(0, T))
        G[pl.ds(base_small + 8 + c, 1), pl.ds(0, WL)] = jnp.sum(g.astype(jnp.float32), axis=0, keepdims=True)
        grad = f32dot(ain[...], g, TN)
        if c < 2:
            G[pl.ds(base_pack, D), pl.ds(c * WL, WL)] = grad
        else:
            for p in range(2):
                G[pl.ds(base_pack + D, WL), pl.ds(p * WL, WL)] = grad[p * WL : (p + 1) * WL, :]
    tick()
    passed(1)

    for h in (0, 1):
        rows = pl.ds(h * half, half)
        acc = f32dot(joined(0, rows), wp[0], NT)
        for c in (1, 2):
            acc = acc + f32dot(joined(c, rows), wp[c], NT)
        PX[1, rows, :] = acc
        swap(3, h).start()

    def input_half(h, totals):
        tick(h)
        swap(3, h).wait()

        def input_rows(i, totals):
            rows = pl.ds(pl.multiple_of(h * half + i * 32, 32), 32)
            g = PX[1, rows, :] + RX[1, rows, :]
            normed, inv = norm(x[rows, :].astype(jnp.float32))
            scaled = g * ag[...]
            v = mid[rows, :] + (scaled - mean_of(scaled) - normed * mean_of(scaled * normed)) * inv
            gi[rows, :] = v.astype(jnp.bfloat16)
            return (
                totals[0] + jnp.sum(g * normed, axis=0, keepdims=True),
                totals[1] + jnp.sum(g, axis=0, keepdims=True),
            )

        return lax.fori_loop(0, half // 32, input_rows, totals)

    sums = lax.fori_loop(0, 2, input_half, (zero, zero))
    passed(2)
    small_row(0)[...] = sums[0]
    small_row(1)[...] = sums[1]
    G[pl.ds(base_small + 8, 3), pl.ds(WL, D - WL)] = jnp.zeros((3, D - WL), jnp.float32)
    G[pl.ds(base_small + 11, SMALL - 11), :] = jnp.zeros((SMALL - 11, D), jnp.float32)

    def body(i, carry):
        comm.step(i)
        comm.small(i - at_step[0], base_small)
        return carry

    lax.fori_loop(at_step[0], comm.steps(), body, 0)


def unpack(moves_of, whole_ref, bo_ref, gi_ref, *refs):
    outs, local = refs[:-1], refs[-1]
    stores = []
    pairs, rows = moves_of(whole_ref, bo_ref, gi_ref, outs)
    for pair in pairs:
        cp = pltpu.make_async_copy(*pair, local.at[len(stores)])
        cp.start()
        stores.append(cp)
    for src, dst in rows:
        dst[...] = src[...]
    for cp in stores:
        cp.wait()


def unpack_moves(T, D, WL, FL, O, bo, gi, outs):
    base_out = FL + D * (FL // D)
    base_pack = base_out + WL
    base_small = base_pack + D + WL
    pairs = [(bo, outs[0]), (gi, outs[1]), (O.at[pl.ds(0, FL), :], outs[2])]
    for p in range(FL // D):
        pairs.append((O.at[pl.ds(FL + p * D, D), :], outs[3].at[:, pl.ds(p * D, D)]))
    pairs.append((O.at[pl.ds(base_out, WL), :], outs[4]))
    for c in range(2):
        pairs.append((O.at[pl.ds(base_pack, D), pl.ds(c * WL, WL)], outs[5].at[c]))
    for p in range(2):
        pairs.append((O.at[pl.ds(base_pack + D, WL), pl.ds(p * WL, WL)], outs[5].at[2, pl.ds(p * WL, WL), :]))
    rows = [(O.at[base_small + k, :], outs[6 + k]) for k in range(6)]
    for p in range(FL // D):
        rows.append((O.at[base_small + 6 + p, :], outs[12].at[pl.ds(p * D, D)]))
    rows.append((O.at[pl.ds(base_small + 8, 3), pl.ds(0, WL)], outs[13]))
    return pairs, rows


def body(
    n_dp,
    block_input,
    sequence_ids,
    attention_gain,
    attention_shift,
    packed_weight,
    packed_bias,
    output_weight,
    output_bias,
    feedforward_gain,
    feedforward_shift,
    expand_weight,
    expand_bias,
    shrink_weight,
    shrink_bias,
    grad_output,
):
    T, D = block_input.shape
    WL = packed_weight.shape[2]
    FL = shrink_weight.shape[0]
    parts = WL // LANES
    bf16, f32 = jnp.bfloat16, jnp.float32
    cosine, sine = tables(T)
    total = FL + D * (FL // D) + WL + D + WL + SMALL

    args = [
        block_input,
        sequence_ids,
        attention_gain,
        attention_shift,
        jnp.transpose(packed_weight, (1, 0, 2)),
        packed_bias,
        output_weight,
        output_bias,
        feedforward_gain,
        feedforward_shift,
        expand_weight,
        expand_bias,
        shrink_weight,
        shrink_bias,
        grad_output,
        jnp.asarray(cosine),
        jnp.asarray(sine),
    ]
    hbm = pl.BlockSpec(memory_space=pltpu.HBM)
    vmem = pl.BlockSpec(memory_space=pltpu.VMEM)
    held = [pltpu.VMEM(a.shape, a.dtype) for a in args]
    scratch = comm_scratch(D)
    whole, out, grad_in = pl.pallas_call(
        functools.partial(layer_kernel, n_dp),
        out_shape=[pltpu.VMEM((total, D), f32), pltpu.VMEM((T, D), bf16), pltpu.VMEM((T, D), bf16)],
        in_specs=[hbm] * 17,
        out_specs=[vmem] * 3,
        scratch_shapes=held
        + [
            pltpu.VMEM((T, D), bf16),
            pltpu.VMEM((3 * parts, T, LANES), bf16),
            pltpu.VMEM((T, WL), bf16),
            pltpu.VMEM((2 * parts, T, T), bf16),
            pltpu.VMEM((T, D), f32),
            pltpu.VMEM((T, D), bf16),
            pltpu.VMEM((T, FL), bf16),
            pltpu.VMEM((2, T, D), f32),
            pltpu.VMEM((2, T, D), f32),
            pltpu.VMEM((3 * parts, T, LANES), bf16),
            pltpu.VMEM((total, D), f32),
        ]
        + scratch[:5]
        + [pltpu.SemaphoreType.DMA((19,)), pltpu.SemaphoreType.DMA((3, 2)), pltpu.SemaphoreType.DMA((3, 2))]
        + [pltpu.SemaphoreType.DMA((T // 128,)), pltpu.SemaphoreType.DMA((T // 128,)), pltpu.VMEM((FL // WL, WL), f32)]
        + scratch[5:],
        compiler_params=pltpu.CompilerParams(
            collective_id=0, has_side_effects=True, vmem_limit_bytes=48 << 20
        ),
    )(*args)
    shapes = [
        ((T, D), bf16),
        ((T, D), bf16),
        ((FL, D), f32),
        ((D, FL), f32),
        ((WL, D), f32),
        ((3, D, WL), f32),
        *[((D,), f32)] * 6,
        ((FL,), f32),
        ((3, WL), f32),
    ]
    anywhere = pl.BlockSpec(memory_space=pl.ANY)
    got = pl.pallas_call(
        functools.partial(unpack, functools.partial(unpack_moves, T, D, WL, FL)),
        out_shape=[pltpu.HBM(*s) for s in shapes[:6]] + [jax.ShapeDtypeStruct(*s) for s in shapes[6:]],
        in_specs=[vmem] * 3,
        out_specs=[anywhere] * 6 + [vmem] * 8,
        scratch_shapes=[pltpu.SemaphoreType.DMA((32,))],
        compiler_params=pltpu.CompilerParams(vmem_limit_bytes=1 << 20),
    )(whole, out, grad_in)
    small = got[6:12]
    return (
        got[0],
        got[1],
        small[0],
        small[1],
        jnp.transpose(got[5], (1, 0, 2)),
        got[13],
        got[4],
        small[2],
        small[3],
        small[4],
        got[3],
        got[12],
        got[2],
        small[5],
    )


def solution(mesh):
    in_specs = (
        P("dp", None),
        P("dp"),
        P(),
        P(),
        P(None, None, "tensor"),
        P(None, "tensor"),
        P("tensor", None),
        P(),
        P(),
        P(),
        P(None, "tensor"),
        P("tensor"),
        P("tensor", None),
        P(),
        P("dp", None),
    )
    out_specs = (
        P("dp", None),
        P("dp", None),
        P(),
        P(),
        P(None, None, "tensor"),
        P(None, "tensor"),
        P("tensor", None),
        P(),
        P(),
        P(),
        P(None, "tensor"),
        P("tensor"),
        P("tensor", None),
        P(),
    )
    return jax.shard_map(
        functools.partial(body, mesh.shape["dp"]), mesh=mesh, in_specs=in_specs, out_specs=out_specs, check_vma=False
    )
```
